32 devices in a mesh: group: 2 (over x), tok: 16 (over z, y, core).
Axes of the slice: x: 2, y: 2, z: 4, core: 2. Of those that a mesh axis runs over, the one named last changes fastest.
Arguments:
- activations: bfloat16 [32768, 1024], P(('group', 'tok')), parts along dimension 0, may hold values from -14 to 14
- view_id: int32 [32768], P(('group', 'tok')), parts along dimension 0, may hold values from 0 to 15, as said below
- window_lengths: int32 [32, 3], P(('group', 'tok')), parts along dimension 0, may hold values from 1 to 512, 1024 in all within a row
- project_weight: bfloat16 [1024, 3072], replicated, may hold values from -0.1875 to 0.1875
- rate_weight: bfloat16 [1024, 4], replicated, may hold values from -0.1875 to 0.1875
- fast_start: float32 [256, 3, 4, 256], replicated, may hold values from -0.375 to 0.375
- momentum: float32 [512, 3, 4, 256], P(('group', 'tok')), parts along dimension 0, may hold values from -0.1875 to 0.1875
- norm_gain: float32 [4, 256], replicated, may hold values from 0.1 to 1.9
- output_weight: bfloat16 [1024, 1024], replicated, may hold values from -0.1875 to 0.1875
Outputs:
- mixed_views: bfloat16 [32, 1024, 1024], P(('group', 'tok')), parts along dimension 0
- momentum_next: float32 [512, 3, 4, 256], P(('group', 'tok')), parts along dimension 0
The draws below stay inside these ranges and needn't reach their ends.
There are 2 independent parts, one for each index of `group`. The reference program is written for one: setup_inputs(seed, part) draws one part's arguments, and reference() takes and returns one part's arrays. A program takes and returns all parts, laid end to end along the dimension named above; an argument that names none is the same for every part. Nothing has to cross between parts.
Inputs may be any that keep to these rules, and one draw needn't show every extreme that they name: `view_id`: each block of 1024 consecutive tokens holds exactly 64 tokens of every view.
All inputs are finite; a program needn't handle non-finite values.
Results may differ from the reference program's by a relative error of at most 0.012.
The reference program's roundings to bfloat16 on the way count: a program that leaves them out, or rounds other values in their place, can miss the bound.
Values may be sent and summed in bfloat16 or wider, within the bound.
No kernel may reach another device: no remote copies, remote signals or barrier semaphores. Data moves between devices by JAX's collectives and lax.ppermute only.
A program may use at most 128 MiB of HBM per device.

```python
import math
import jax
import jax.numpy as jnp
import numpy as np
from jax import lax

D = 1024
H = 4
HD = 256
FI = 256
TOK_DEV = 1024
WINDOW = 512
WINS = 3
VIEWS = 16
TOKENS = 16384


def draw_activations(key, part):
    values = jax.random.truncated_normal(key, -6.0, 6.0, (TOKENS, D), jnp.float32)
    return values.astype(jnp.bfloat16)


def draw_view_id(key, part):
    blocks = TOKENS // TOK_DEV
    pattern = (jnp.arange(TOK_DEV, dtype=jnp.int32) % VIEWS).astype(jnp.int32)
    block_keys = jax.random.split(jax.random.fold_in(key, 5), blocks)
    shuffled = jax.vmap(lambda block_key: jax.random.permutation(block_key, pattern))(block_keys)
    return shuffled.reshape(TOKENS).astype(jnp.int32)


def block_levels(key, shape, cuts, smallest, high):
    factor_of, own = 1.0, jax.random.fold_in(key, 6)
    for position, parts in cuts:
        steps = jnp.exp(jax.random.uniform(jax.random.fold_in(own, position), (parts,), jnp.float32, smallest / len(cuts), high / len(cuts)))
        factor_of = factor_of * jnp.repeat(steps, shape[position] // parts).reshape([-1 if axis == position else 1 for axis in range(len(shape))])
    return factor_of


def split_up(number_of, total, most, skew):
    loads = [(1 << 20) // math.isqrt(standing ** skew) + 1 for standing in range(2, number_of + 1)]
    rest, holding = total - most - (number_of - 1), [1] * (number_of - 1)
    while rest > 0:
        free = [i for i in range(number_of - 1) if holding[i] < most]
        mass, remaining = sum([loads[i] for i in free]), rest
        for i in free:
            more = min(most - holding[i], max(1, remaining * loads[i] // mass), rest)
            holding[i] = holding[i] + more
            rest = rest - more
    return np.array([most] + holding)


def ragged_sizes(own_key, number_of, total, reach, lean):
    if number_of == 2:
        one = jax.random.randint(own_key, (), max(1, total - reach), min(reach, total - 1) + 1)
        return jnp.stack([one, total - one])
    tallies = jnp.asarray(split_up(number_of, total, reach, lean), jnp.int32)
    pairs = (number_of - 1) // 2
    donor, sink = tallies[1:1 + 2 * pairs:2], tallies[2:2 + 2 * pairs:2]
    margin = jnp.minimum(donor - 1, reach - sink)
    passed = jax.random.randint(jax.random.fold_in(own_key, 1), (pairs,), 0, 1 << 20) % (margin + 1)
    tallies = tallies.at[1:1 + 2 * pairs:2].set(donor - passed).at[2:2 + 2 * pairs:2].set(sink + passed)
    return tallies[jax.random.permutation(jax.random.fold_in(own_key, 2), number_of)]


def bell_draw(own_key, extent, deviation, bound, cuts=(), kind=jnp.bfloat16):
    entries = jax.random.normal(own_key, extent, jnp.float32) * deviation
    if len(cuts) > 0:
        entries = block_levels(own_key, extent, cuts, -0.22, 0.18) * entries
    return jnp.clip(entries, min=-bound, max=bound).astype(kind)


def setup_inputs(seed: int = 0, part: int = 0) -> dict:
    key_of = jax.random.split(jax.random.key(seed), 10)
    own_keys = jax.random.split(jax.random.fold_in(key_of[9], part), 10)
    return {
        "activations": draw_activations(jax.random.fold_in(jax.random.fold_in(key_of[9], part), 71), part),
        "view_id": draw_view_id(jax.random.fold_in(jax.random.fold_in(key_of[9], part), 71), part),
        "window_lengths": jax.vmap(lambda own: ragged_sizes(own, WINS, TOK_DEV, WINDOW, 0))(jax.random.split(own_keys[2], VIEWS)).reshape((VIEWS, WINS)).astype(jnp.int32),
        "project_weight": bell_draw(key_of[3], (D, 3 * D), D ** -0.5, 0.1875),
        "rate_weight": bell_draw(key_of[4], (D, H), D ** -0.5, 0.1875),
        "fast_start": bell_draw(key_of[5], (HD, 3, H, FI), HD ** -0.5, 0.375, (), jnp.float32),
        "momentum": bell_draw(own_keys[6], (HD, 3, H, FI), 0.03, 0.1875, ((0, 16),), jnp.float32),
        "norm_gain": jnp.clip(1.0 + 0.18 * jax.random.normal(key_of[7], (H, HD), jnp.float32), 0.1, 1.9),
        "output_weight": bell_draw(key_of[8], (D, D), D ** -0.5, 0.1875),
    }


def rounded(values):
    return lax.optimization_barrier(values.astype(jnp.bfloat16)).astype(jnp.float32)

def unit_rms(values):
    return values * lax.rsqrt(lax.optimization_barrier(jnp.mean(values * values, axis=-1, keepdims=True)) + 1e-06)

def view_attention(pieces):
    triple, lengths = pieces
    queries = triple[:, :D].astype(jnp.float32).reshape(TOK_DEV, H, HD)
    keys_all = triple[:, D:2 * D].astype(jnp.float32).reshape(TOK_DEV, H, HD)
    values_all = triple[:, 2 * D:].astype(jnp.float32).reshape(TOK_DEV, H, HD)
    bounds = jnp.cumsum(lengths)
    window_of = lax.optimization_barrier(jnp.sum(jnp.arange(TOK_DEV)[:, None] >= bounds[None, :], axis=1))
    scores = jnp.einsum('qhd,khd->hqk', queries, keys_all) / math.sqrt(HD)
    same = window_of[:, None] == window_of[None, :]
    scores = jnp.where(same[None], scores, -1e+30)
    highest = lax.optimization_barrier(jnp.max(scores, axis=-1, keepdims=True))
    expo = jnp.exp(scores - highest)
    probs = rounded(expo / lax.optimization_barrier(jnp.sum(expo, axis=-1, keepdims=True)))
    return jnp.einsum('hqk,khd->qhd', probs, values_all).reshape(TOK_DEV, D)

def reference(activations, view_id, window_lengths, project_weight, rate_weight, fast_start, momentum, norm_gain, output_weight):
    f32 = jnp.float32
    projected_raw = jnp.dot(activations, project_weight, preferred_element_type=f32).astype(jnp.bfloat16)
    projected = lax.optimization_barrier(projected_raw)
    queries = projected[:, :D].astype(f32).reshape(TOKENS, H, HD)
    keys_all = projected[:, D:2 * D].astype(f32).reshape(TOKENS, H, HD)
    values_all = projected[:, 2 * D:].astype(f32).reshape(TOKENS, H, HD)
    rate = jax.nn.softplus(jnp.dot(activations, rate_weight, preferred_element_type=f32)) * (0.1 / math.sqrt(TOKENS))
    key_unit = rounded(unit_rms(keys_all))
    fast_round = rounded(fast_start)
    pre_gate = jnp.einsum('thd,dhf->thf', key_unit, fast_round[:, 0])
    pre_up = jnp.einsum('thd,dhf->thf', key_unit, fast_round[:, 1])
    gate_sig = jax.nn.sigmoid(pre_gate)
    hidden = rounded(pre_gate * gate_sig * pre_up)
    back_out = rounded(-rate[:, :, None] * values_all)
    back_hidden = jnp.einsum('thd,dhf->thf', back_out, fast_round[:, 2])
    back_gate = rounded(back_hidden * pre_up * gate_sig * (1.0 + pre_gate * (1.0 - gate_sig)))
    back_up = rounded(back_hidden * pre_gate * gate_sig)
    grad_gate = jnp.einsum('thr,thf->rhf', key_unit, back_gate)
    grad_up = jnp.einsum('thr,thf->rhf', key_unit, back_up)
    grad_down = jnp.einsum('thr,thf->rhf', back_out, hidden)
    gradient = jnp.stack([grad_gate, grad_up, grad_down], axis=1)
    momentum_next = 0.9 * momentum + gradient
    moved = fast_start - momentum_next
    factor = jnp.sqrt(lax.optimization_barrier(jnp.sum(fast_start * fast_start, axis=-1, keepdims=True))) / jnp.sqrt(lax.optimization_barrier(jnp.sum(moved * moved, axis=-1, keepdims=True)) + 1e-06)
    fast_new = rounded(moved * factor)
    query_unit = rounded(unit_rms(queries))
    query_gate = jnp.einsum('thd,dhf->thf', query_unit, fast_new[:, 0])
    query_up = jnp.einsum('thd,dhf->thf', query_unit, fast_new[:, 1])
    query_hidden = rounded(query_gate * jax.nn.sigmoid(query_gate) * query_up)
    fast_out = jnp.einsum('thf,dhf->thd', query_hidden, fast_new[:, 2])
    normed = (unit_rms(fast_out) * norm_gain[None]).reshape(TOKENS, D).astype(jnp.bfloat16)
    ordering = jnp.argsort(view_id, stable=True).astype(jnp.int32)
    grouped = projected[ordering].reshape(VIEWS, TOK_DEV, 3 * D)
    normed_views = normed[ordering].reshape(VIEWS, TOK_DEV, D)
    attended = lax.map(view_attention, (grouped, window_lengths))
    combined = (normed_views.astype(f32) + attended).astype(jnp.bfloat16)
    mixed = jnp.dot(combined.reshape(TOKENS, D), output_weight, preferred_element_type=f32)
    return (mixed.astype(jnp.bfloat16).reshape(VIEWS, TOK_DEV, D), momentum_next)
```

```python
import math

import jax
import jax.numpy as jnp
from jax import lax
from jax.experimental import pallas as pl
from jax.experimental.pallas import tpu as pltpu
from jax.sharding import PartitionSpec as P

F32 = jnp.float32
BF16 = jnp.bfloat16
VMEM_LIMIT = 60 * 1024 * 1024


def dot(a, b):
    return jnp.dot(a, b, preferred_element_type=F32)


def dot_tn(a, b):
    return lax.dot_general(a, b, (((0,), (0,)), ((), ())), preferred_element_type=F32)


def dot_nt(a, b):
    return lax.dot_general(a, b, (((1,), (1,)), ((), ())), preferred_element_type=F32)


def bit_reverse(value, width):
    out = 0
    for bit in range(width):
        out |= ((value >> bit) & 1) << (width - 1 - bit)
    return out


def params(grid_rank=1):
    return pltpu.CompilerParams(
        dimension_semantics=("arbitrary",) * grid_rank, vmem_limit_bytes=VMEM_LIMIT
    )


def cost(flops, nbytes, transcendentals=0):
    return pl.CostEstimate(
        flops=int(flops), bytes_accessed=int(nbytes), transcendentals=int(transcendentals)
    )


def group_by_view(view_id, activations, shards):
    tok_dev, width = activations.shape
    per_view = tok_dev // shards
    chunk = 256
    tile = 256

    def kernel(view_ref, act_ref, out_ref, slot_ref):
        @pl.when(pl.program_id(0) == 0)
        def _():
            rows = lax.broadcasted_iota(jnp.int32, (chunk, chunk), 0)
            cols = lax.broadcasted_iota(jnp.int32, (chunk, chunk), 1)
            upper = jnp.where(rows < cols, 1.0, 0.0).astype(BF16)
            views = lax.broadcasted_iota(jnp.int32, (shards, chunk), 0)
            before = jnp.zeros((shards, 1), F32)
            for start in range(0, tok_dev, chunk):
                member = views == view_ref[:, start : start + chunk]
                hot = jnp.where(member, 1.0, 0.0)
                rank = dot(hot.astype(BF16), upper) + before
                slot = jnp.where(member, rank + (views * per_view).astype(F32), 0.0)
                slot_ref[:, start : start + chunk] = jnp.sum(slot, axis=0, keepdims=True).astype(
                    jnp.int32
                )
                before = before + jnp.sum(hot, axis=1, keepdims=True)

        target = lax.broadcasted_iota(jnp.int32, (tile, tok_dev), 0) + pl.program_id(0) * tile
        pick = jnp.where(target == slot_ref[...], 1.0, 0.0).astype(BF16)
        out_ref[...] = dot(pick, act_ref[...]).astype(BF16)

    return pl.pallas_call(
        kernel,
        grid=(tok_dev // tile,),
        in_specs=[
            pl.BlockSpec((1, tok_dev), lambda i: (0, 0)),
            pl.BlockSpec((tok_dev, width), lambda i: (0, 0)),
        ],
        out_specs=pl.BlockSpec((tile, width), lambda i: (i, 0)),
        out_shape=jax.ShapeDtypeStruct((tok_dev, width), BF16),
        scratch_shapes=[pltpu.VMEM((1, tok_dev), jnp.int32)],
        compiler_params=params(),
        cost_estimate=cost(2 * tok_dev * tok_dev * width, 4 * tok_dev * width),
        name="group_by_view",
    )(view_id.reshape(1, tok_dev), activations)


def fast_gradient(position, activations, project_weight, rate_weight, fast_round, shards):
    tok_dev, width = activations.shape
    heads = rate_weight.shape[1]
    size = width // heads
    slab = size // shards
    stages = shards.bit_length() - 1
    tile = 256
    scale = 0.1 / math.sqrt(tok_dev * shards)
    half = size // 2

    def kernel(pos_ref, act_ref, wk_ref, wv_ref, rate_w_ref, fast_ref, keep_ref, send_ref,
               rate_ref, key_ref, out_ref, hid_ref, gate_ref, grad_ref):
        head = pl.program_id(0)

        @pl.when(head == 0)
        def _():
            raw = dot(act_ref[...], rate_w_ref[...])
            rate_ref[...] = (jnp.maximum(raw, 0.0) + jnp.log1p(jnp.exp(-jnp.abs(raw)))) * scale

        w_gate = fast_ref[:, 0:size]
        w_up = fast_ref[:, size : 2 * size]
        w_down = fast_ref[:, 2 * size : 3 * size]
        for start in range(0, tok_dev, tile):
            rows = slice(start, start + tile)
            act = act_ref[rows, :]
            keys = dot(act, wk_ref[...]).astype(BF16).astype(F32)
            values = dot(act, wv_ref[...]).astype(BF16).astype(F32)
            key_unit = (
                keys * lax.rsqrt(jnp.mean(keys * keys, axis=-1, keepdims=True) + 1e-06)
            ).astype(BF16)
            lanes = lax.broadcasted_iota(jnp.int32, (tile, heads), 1)
            rate = jnp.sum(
                jnp.where(lanes == head, rate_ref[rows, :], 0.0), axis=1, keepdims=True
            )
            back_out = (-rate * values).astype(BF16)
            pre_gate = dot(key_unit, w_gate)
            pre_up = dot(key_unit, w_up)
            back_hidden = dot(back_out, w_down)
            sig = jax.nn.sigmoid(pre_gate)
            act_gate = pre_gate * sig
            key_ref[rows, :] = key_unit
            out_ref[rows, :] = back_out
            hid_ref[rows, :] = (act_gate * pre_up).astype(BF16)
            gate_ref[rows, 0:size] = (
                back_hidden * pre_up * sig * (1.0 + pre_gate * (1.0 - sig))
            ).astype(BF16)
            gate_ref[rows, size : 2 * size] = (back_hidden * act_gate).astype(BF16)
        grad_ref[:, 0 : 2 * size] = dot_tn(key_ref[...], gate_ref[...])
        grad_ref[:, 2 * size : 3 * size] = dot_tn(out_ref[...], hid_ref[...])
        for place in range(shards):
            owner = pos_ref[0] ^ bit_reverse(place, stages)
            rows = grad_ref[pl.ds(pl.multiple_of(owner * slab, slab), slab), :]
            if place < shards // 2:
                keep_ref[place * slab : (place + 1) * slab, :] = rows
            else:
                low = place * slab - half
                send_ref[low : low + slab, :] = rows.astype(BF16)

    return pl.pallas_call(
        kernel,
        grid_spec=pltpu.PrefetchScalarGridSpec(
            num_scalar_prefetch=1,
            grid=(heads,),
            in_specs=[
                pl.BlockSpec((tok_dev, width), lambda h, p: (0, 0)),
                pl.BlockSpec((width, size), lambda h, p: (0, heads + h)),
                pl.BlockSpec((width, size), lambda h, p: (0, 2 * heads + h)),
                pl.BlockSpec((width, heads), lambda h, p: (0, 0)),
                pl.BlockSpec((size, 3 * size), lambda h, p: (0, h)),
            ],
            out_specs=[
                pl.BlockSpec((half, 3 * size), lambda h, p: (0, h)),
                pl.BlockSpec((half, 3 * size), lambda h, p: (0, h)),
            ],
            scratch_shapes=[
                pltpu.VMEM((tok_dev, heads), F32),
                pltpu.VMEM((tok_dev, size), BF16),
                pltpu.VMEM((tok_dev, size), BF16),
                pltpu.VMEM((tok_dev, size), BF16),
                pltpu.VMEM((tok_dev, 2 * size), BF16),
                pltpu.VMEM((size, 3 * size), F32),
            ],
        ),
        out_shape=[
            jax.ShapeDtypeStruct((half, 3 * width), F32),
            jax.ShapeDtypeStruct((half, 3 * width), BF16),
        ],
        compiler_params=params(),
        cost_estimate=cost(
            2 * tok_dev * width * (2 * width + 6 * size),
            2 * tok_dev * width + 4 * width * width + 6 * size * width + 9 * size * width,
            4 * tok_dev * width,
        ),
        name="fast_gradient",
    )(position, activations, project_weight, project_weight, rate_weight, fast_round)


def add_and_halve(keep, received):
    rows, width = keep.shape
    half = rows // 2
    cols = width // 4

    def kernel(keep_ref, got_ref, stay_ref, go_ref):
        total = keep_ref[...] + got_ref[...].astype(F32)
        stay_ref[...] = total[:half]
        go_ref[...] = total[half:].astype(BF16)

    return pl.pallas_call(
        kernel,
        grid=(4,),
        in_specs=[pl.BlockSpec((rows, cols), lambda i: (0, i))] * 2,
        out_specs=[pl.BlockSpec((half, cols), lambda i: (0, i))] * 2,
        out_shape=[
            jax.ShapeDtypeStruct((half, width), F32),
            jax.ShapeDtypeStruct((half, width), BF16),
        ],
        compiler_params=params(),
        cost_estimate=cost(rows * width, 9 * rows * width),
        name="add_and_halve",
    )(keep, received)


def update_rows(keep, received, momentum, own_start, size):
    rows, width = keep.shape

    def kernel(keep_ref, got_ref, mom_ref, start_ref, next_ref, share_ref):
        for low in range(0, width, size):
            cols = slice(low, low + size)
            moment = 0.9 * mom_ref[:, cols] + (keep_ref[:, cols] + got_ref[:, cols].astype(F32))
            next_ref[:, cols] = moment
            start = start_ref[:, cols]
            moved = start - moment
            factor = jnp.sqrt(jnp.sum(start * start, axis=-1, keepdims=True)) / jnp.sqrt(
                jnp.sum(moved * moved, axis=-1, keepdims=True) + 1e-06
            )
            share_ref[:, cols] = (moved * factor).astype(BF16)

    return pl.pallas_call(
        kernel,
        out_shape=[
            jax.ShapeDtypeStruct((rows, width), F32),
            jax.ShapeDtypeStruct((rows, width), BF16),
        ],
        cost_estimate=cost(8 * rows * width, 20 * rows * width),
        name="update_rows",
    )(keep, received, momentum, own_start)


def project_and_attend(window_ends, arrived, project_weight, heads):
    tok_dev, width = arrived.shape
    size = width // heads
    windows = window_ends.shape[0]
    tile = 256
    scale = 1.0 / math.sqrt(size)

    def kernel(ends_ref, x_ref, wq_ref, wk_ref, wv_ref, unit_ref, att_ref):
        x = x_ref[...]
        queries = dot(x, wq_ref[...]).astype(BF16)
        keys = dot(x, wk_ref[...]).astype(BF16)
        values = dot(x, wv_ref[...]).astype(BF16)
        wide = queries.astype(F32)
        unit_ref[...] = (
            wide * lax.rsqrt(jnp.mean(wide * wide, axis=-1, keepdims=True) + 1e-06)
        ).astype(BF16)
        key_place = lax.broadcasted_iota(jnp.int32, (1, tok_dev), 1)
        key_window = jnp.zeros((1, tok_dev), jnp.int32)
        for w in range(windows):
            key_window += (key_place >= ends_ref[w]).astype(jnp.int32)
        for start in range(0, tok_dev, tile):
            place = lax.broadcasted_iota(jnp.int32, (tile, 1), 0) + start
            window = jnp.zeros((tile, 1), jnp.int32)
            for w in range(windows):
                window += (place >= ends_ref[w]).astype(jnp.int32)
            scores = dot_nt(queries[start : start + tile], keys) * scale
            scores = jnp.where(window == key_window, scores, -1e30)
            highest = jnp.max(scores, axis=-1, keepdims=True)
            expo = jnp.exp(scores - highest)
            total = jnp.sum(expo, axis=-1, keepdims=True)
            att_ref[start : start + tile, :] = dot(expo.astype(BF16), values) / total

    return pl.pallas_call(
        kernel,
        grid_spec=pltpu.PrefetchScalarGridSpec(
            num_scalar_prefetch=1,
            grid=(heads,),
            in_specs=[
                pl.BlockSpec((tok_dev, width), lambda h, e: (0, 0)),
                pl.BlockSpec((width, size), lambda h, e: (0, h)),
                pl.BlockSpec((width, size), lambda h, e: (0, heads + h)),
                pl.BlockSpec((width, size), lambda h, e: (0, 2 * heads + h)),
            ],
            out_specs=[
                pl.BlockSpec((tok_dev, size), lambda h, e: (0, h)),
                pl.BlockSpec((tok_dev, size), lambda h, e: (0, h)),
            ],
        ),
        out_shape=[
            jax.ShapeDtypeStruct((tok_dev, width), BF16),
            jax.ShapeDtypeStruct((tok_dev, width), F32),
        ],
        compiler_params=params(),
        cost_estimate=cost(
            2 * tok_dev * width * (3 * width + 2 * tok_dev),
            8 * tok_dev * width + 6 * width * width,
            heads * tok_dev * tok_dev,
        ),
        name="project_and_attend",
    )(window_ends, arrived, project_weight, project_weight, project_weight)


def apply_fast(position, gathered, unit, attended, norm_gain, output_weight, shards):
    tok_dev, width = unit.shape
    heads, size = norm_gain.shape
    slab = size // shards
    stages = shards.bit_length() - 1
    tile = 256
    parts = len(gathered)
    part_rows = size // parts

    def kernel(pos_ref, *refs):
        part_refs = refs[:parts]
        unit_ref, att_ref, gain_ref, ow_ref, mix_ref, wide_ref, fast_ref = refs[parts:]

        @pl.when(pl.program_id(0) == 0)
        def _():
            for place in range(shards):
                owner = pos_ref[0] ^ bit_reverse(place, stages)
                low = (place * slab) % part_rows
                rows = part_refs[place * slab // part_rows][low : low + slab, :]
                wide_ref[pl.ds(pl.multiple_of(owner * slab, slab), slab), :] = rows.astype(F32)
            fast_ref[...] = wide_ref[...].astype(BF16)

        pieces = []
        for head in range(heads):
            low = head * 3 * size
            cols = slice(head * size, (head + 1) * size)
            query = unit_ref[:, cols]
            gate = dot(query, fast_ref[:, low : low + size])
            up = dot(query, fast_ref[:, low + size : low + 2 * size])
            hidden = (gate * jax.nn.sigmoid(gate) * up).astype(BF16)
            out = dot_nt(hidden, fast_ref[:, low + 2 * size : low + 3 * size])
            out = out * lax.rsqrt(jnp.mean(out * out, axis=-1, keepdims=True) + 1e-06)
            normed = (out * gain_ref[head : head + 1, :]).astype(BF16).astype(F32)
            pieces.append((normed + att_ref[:, cols]).astype(BF16))
        combined = jnp.concatenate(pieces, axis=1)
        mix_ref[...] = dot(combined, ow_ref[...]).astype(BF16)

    return pl.pallas_call(
        kernel,
        grid_spec=pltpu.PrefetchScalarGridSpec(
            num_scalar_prefetch=1,
            grid=(tok_dev // tile,),
            in_specs=[pl.BlockSpec((part_rows, 3 * width), lambda i, p: (0, 0))] * parts
            + [
                pl.BlockSpec((tile, width), lambda i, p: (i, 0)),
                pl.BlockSpec((tile, width), lambda i, p: (i, 0)),
                pl.BlockSpec((heads, size), lambda i, p: (0, 0)),
                pl.BlockSpec((width, width), lambda i, p: (0, 0)),
            ],
            out_specs=pl.BlockSpec((tile, width), lambda i, p: (i, 0)),
            scratch_shapes=[
                pltpu.VMEM((size, 3 * width), F32),
                pltpu.VMEM((size, 3 * width), BF16),
            ],
        ),
        out_shape=jax.ShapeDtypeStruct((tok_dev, width), BF16),
        compiler_params=params(),
        cost_estimate=cost(
            2 * tok_dev * width * (width + 3 * size),
            8 * tok_dev * width + 2 * width * width + 6 * size * width,
            tok_dev * width,
        ),
        name="apply_fast",
    )(position, *gathered, unit, attended, norm_gain, output_weight)


def body(
    activations,
    view_id,
    window_lengths,
    project_weight,
    rate_weight,
    fast_start,
    momentum,
    norm_gain,
    output_weight,
):
    tok_dev, width = activations.shape
    shards = lax.axis_size("tok")
    index = lax.axis_index("tok")
    position = index.reshape(1).astype(jnp.int32)
    heads = rate_weight.shape[1]
    size = width // heads
    slab = size // shards

    def swap(array, bit):
        return lax.ppermute(array, "tok", [(i, i ^ bit) for i in range(shards)])

    def flat(array):
        return jnp.swapaxes(array, 1, 2).reshape(array.shape[0], 3 * width)

    sent = group_by_view(view_id, activations, shards)
    arrived = lax.all_to_all(
        sent.reshape(shards, tok_dev // shards, width), "tok", split_axis=0, concat_axis=0, tiled=True
    ).reshape(tok_dev, width)

    fast_round = flat(fast_start.astype(BF16))
    own_start = flat(lax.dynamic_slice_in_dim(fast_start, index * slab, slab, 0))
    keep, send = fast_gradient(
        position, activations, project_weight, rate_weight, fast_round, shards
    )
    bit = 1
    while bit < shards:
        received = swap(send, bit)
        bit *= 2
        if bit < shards:
            keep, send = add_and_halve(keep, received)
    moment, share = update_rows(keep, received, flat(momentum), own_start, size)
    momentum_next = jnp.swapaxes(moment.reshape(slab, heads, 3, size), 1, 2)

    unit, attended = project_and_attend(
        jnp.cumsum(window_lengths[0]), arrived, project_weight, heads
    )

    bit = shards // 2
    block = share
    while bit > 1:
        block = jnp.concatenate([block, swap(block, bit)], axis=0)
        bit //= 2
    gathered = [block, swap(block, 1)]
    mixed = apply_fast(position, gathered, unit, attended, norm_gain, output_weight, shards)
    return (mixed[None], momentum_next)


def solution(mesh):
    in_specs = (
        P(("group", "tok"), None),
        P(("group", "tok")),
        P(("group", "tok"), None),
        P(),
        P(),
        P(),
        P(("group", "tok"), None, None, None),
        P(),
        P(),
    )
    out_specs = (P(("group", "tok"), None, None), P(("group", "tok"), None, None, None))
    return jax.shard_map(body, mesh=mesh, in_specs=in_specs, out_specs=out_specs, check_vma=False)
```

```python
import math

import jax
import jax.numpy as jnp
from jax import lax
from jax.experimental import pallas as pl
from jax.experimental.pallas import tpu as pltpu
from jax.sharding import PartitionSpec as P

F32 = jnp.float32
BF16 = jnp.bfloat16
MIB = 1024 * 1024


def dot(a, b):
    return jnp.dot(a, b, preferred_element_type=F32)


def dot_tn(a, b):
    return lax.dot_general(a, b, (((0,), (0,)), ((), ())), preferred_element_type=F32)


def dot_nt(a, b):
    return lax.dot_general(a, b, (((1,), (1,)), ((), ())), preferred_element_type=F32)


def bit_reverse(value, width):
    out = 0
    for bit in range(width):
        out |= ((value >> bit) & 1) << (width - 1 - bit)
    return out


def params(mebibytes):
    return pltpu.CompilerParams(
        dimension_semantics=("arbitrary",), vmem_limit_bytes=mebibytes * MIB
    )


def after(array, *others):
    return lax.optimization_barrier((array, *others))[0]


def cost(flops, nbytes, transcendentals=0):
    return pl.CostEstimate(
        flops=int(flops), bytes_accessed=int(nbytes), transcendentals=int(transcendentals)
    )


def group_by_view(view_id, activations, shards):
    tok_dev, width = activations.shape
    per_view = tok_dev // shards
    chunk = 256
    tile = 256

    def kernel(view_ref, act_ref, out_ref, slot_ref):
        @pl.when(pl.program_id(0) == 0)
        def _():
            rows = lax.broadcasted_iota(jnp.int32, (chunk, chunk), 0)
            cols = lax.broadcasted_iota(jnp.int32, (chunk, chunk), 1)
            upper = jnp.where(rows < cols, 1.0, 0.0).astype(BF16)
            views = lax.broadcasted_iota(jnp.int32, (shards, chunk), 0)
            before = jnp.zeros((shards, 1), F32)
            for start in range(0, tok_dev, chunk):
                member = views == view_ref[:, start : start + chunk]
                hot = jnp.where(member, 1.0, 0.0)
                rank = dot(hot.astype(BF16), upper) + before
                slot = jnp.where(member, rank + (views * per_view).astype(F32), 0.0)
                slot_ref[:, start : start + chunk] = jnp.sum(slot, axis=0, keepdims=True).astype(
                    jnp.int32
                )
                before = before + jnp.sum(hot, axis=1, keepdims=True)

        target = lax.broadcasted_iota(jnp.int32, (tile, tok_dev), 0) + pl.program_id(0) * tile
        pick = jnp.where(target == slot_ref[...], 1.0, 0.0).astype(BF16)
        out_ref[...] = dot(pick, act_ref[...]).astype(BF16)

    return pl.pallas_call(
        kernel,
        grid=(tok_dev // tile,),
        in_specs=[
            pl.BlockSpec((1, tok_dev), lambda i: (0, 0)),
            pl.BlockSpec((tok_dev, width), lambda i: (0, 0)),
        ],
        out_specs=pl.BlockSpec((tile, width), lambda i: (i, 0)),
        out_shape=jax.ShapeDtypeStruct((tok_dev, width), BF16),
        scratch_shapes=[pltpu.VMEM((1, tok_dev), jnp.int32)],
        compiler_params=params(60),
        cost_estimate=cost(2 * tok_dev * tok_dev * width, 4 * tok_dev * width),
        name="group_by_view",
    )(view_id.reshape(1, tok_dev), activations)


def fast_gradient(position, activations, project_weight, rate_weight, fast_start, shards):
    tok_dev, width = activations.shape
    heads = rate_weight.shape[1]
    kinds = fast_start.shape[1]
    size = width // heads
    slab = size // shards
    stages = shards.bit_length() - 1
    tile = 256
    scale = 0.1 / math.sqrt(tok_dev * shards)
    half = size // 2

    def kernel(pos_ref, act_ref, wk_ref, wv_ref, rate_w_ref, fast_ref, keep_ref, send_ref,
               rate_ref, key_ref, out_ref, hid_ref, gate_ref, grad_ref, start_ref, sems):
        head = pl.program_id(0)
        slot = head % 2

        def fetch(which, place):
            return [
                pltpu.make_async_copy(
                    fast_ref.at[:, kind, which, :], start_ref.at[place, kind], sems.at[place, kind]
                )
                for kind in range(kinds)
            ]

        @pl.when(head == 0)
        def _():
            for copy in fetch(0, 0):
                copy.start()
            raw = dot_nt(act_ref[...], rate_w_ref[...])
            rate_ref[...] = (jnp.maximum(raw, 0.0) + jnp.log1p(jnp.exp(-jnp.abs(raw)))) * scale

        @pl.when(head + 1 < heads)
        def _():
            for copy in fetch(head + 1, 1 - slot):
                copy.start()

        for copy in fetch(head, slot):
            copy.wait()
        w_gate, w_up, w_down = [start_ref[slot, kind].astype(BF16) for kind in range(kinds)]
        for start in range(0, tok_dev, tile):
            rows = slice(start, start + tile)
            act = act_ref[rows, :]
            keys = dot(act, wk_ref[...]).astype(BF16).astype(F32)
            values = dot(act, wv_ref[...]).astype(BF16).astype(F32)
            key_unit = (
                keys * lax.rsqrt(jnp.mean(keys * keys, axis=-1, keepdims=True) + 1e-06)
            ).astype(BF16)
            lanes = lax.broadcasted_iota(jnp.int32, (tile, heads), 1)
            rate = jnp.sum(
                jnp.where(lanes == head, rate_ref[rows, :], 0.0), axis=1, keepdims=True
            )
            back_out = (-rate * values).astype(BF16)
            pre_gate = dot(key_unit, w_gate)
            pre_up = dot(key_unit, w_up)
            back_hidden = dot(back_out, w_down)
            sig = jax.nn.sigmoid(pre_gate)
            act_gate = pre_gate * sig
            key_ref[rows, :] = key_unit
            out_ref[rows, :] = back_out
            hid_ref[rows, :] = (act_gate * pre_up).astype(BF16)
            gate_ref[rows, 0:size] = (
                back_hidden * pre_up * sig * (1.0 + pre_gate * (1.0 - sig))
            ).astype(BF16)
            gate_ref[rows, size : 2 * size] = (back_hidden * act_gate).astype(BF16)
        grad_ref[:, 0 : 2 * size] = dot_tn(key_ref[...], gate_ref[...])
        grad_ref[:, 2 * size : 3 * size] = dot_tn(out_ref[...], hid_ref[...])
        for place in range(shards):
            owner = pos_ref[0] ^ bit_reverse(place, stages)
            rows = grad_ref[pl.ds(pl.multiple_of(owner * slab, slab), slab), :]
            if place < shards // 2:
                keep_ref[place * slab : (place + 1) * slab, :] = rows
            else:
                low = place * slab - half
                send_ref[low : low + slab, :] = rows.astype(BF16)

    return pl.pallas_call(
        kernel,
        grid_spec=pltpu.PrefetchScalarGridSpec(
            num_scalar_prefetch=1,
            grid=(heads,),
            in_specs=[
                pl.BlockSpec((tok_dev, width), lambda h, p: (0, 0)),
                pl.BlockSpec((width, size), lambda h, p: (0, heads + h)),
                pl.BlockSpec((width, size), lambda h, p: (0, 2 * heads + h)),
                pl.BlockSpec((heads, width), lambda h, p: (0, 0)),
                pl.BlockSpec(memory_space=pl.ANY),
            ],
            out_specs=[
                pl.BlockSpec((half, 3 * size), lambda h, p: (0, h)),
                pl.BlockSpec((half, 3 * size), lambda h, p: (0, h)),
            ],
            scratch_shapes=[
                pltpu.VMEM((tok_dev, heads), F32),
                pltpu.VMEM((tok_dev, size), BF16),
                pltpu.VMEM((tok_dev, size), BF16),
                pltpu.VMEM((tok_dev, size), BF16),
                pltpu.VMEM((tok_dev, 2 * size), BF16),
                pltpu.VMEM((size, 3 * size), F32),
                pltpu.VMEM((2, kinds, size, size), F32),
                pltpu.SemaphoreType.DMA((2, kinds)),
            ],
        ),
        out_shape=[
            jax.ShapeDtypeStruct((half, 3 * width), F32),
            jax.ShapeDtypeStruct((half, 3 * width), BF16),
        ],
        compiler_params=params(60),
        cost_estimate=cost(
            2 * tok_dev * width * (2 * width + 6 * size),
            2 * tok_dev * width + 4 * width * width + 6 * size * width + 9 * size * width,
            4 * tok_dev * width,
        ),
        name="fast_gradient",
    )(position, activations, project_weight, project_weight, rate_weight.T, fast_start)


def add_and_halve(keep, received):
    rows, width = keep.shape
    half = rows // 2

    def kernel(keep_ref, got_ref, stay_ref, go_ref):
        stay_ref[...] = keep_ref[:half, :] + got_ref[:half, :].astype(F32)
        go_ref[...] = (keep_ref[half:, :] + got_ref[half:, :].astype(F32)).astype(BF16)

    whole = pl.BlockSpec(memory_space=pltpu.VMEM)
    return pl.pallas_call(
        kernel,
        in_specs=[whole, whole],
        out_specs=[whole, whole],
        out_shape=[
            jax.ShapeDtypeStruct((half, width), F32),
            jax.ShapeDtypeStruct((half, width), BF16),
        ],
        compiler_params=pltpu.CompilerParams(vmem_limit_bytes=6 * MIB),
        cost_estimate=cost(rows * width, 9 * rows * width),
        name="add_and_halve",
    )(keep, received)


def join(first, second):
    rows, width = first.shape

    def kernel(first_ref, second_ref, out_ref):
        out_ref[:rows, :] = first_ref[...]
        out_ref[rows:, :] = second_ref[...]

    whole = pl.BlockSpec(memory_space=pltpu.VMEM)
    return pl.pallas_call(
        kernel,
        in_specs=[whole, whole],
        out_specs=whole,
        out_shape=jax.ShapeDtypeStruct((2 * rows, width), BF16),
        compiler_params=pltpu.CompilerParams(vmem_limit_bytes=4 * MIB),
        cost_estimate=cost(0, 8 * rows * width),
        name="join",
    )(first, second)


def update_rows(keep, received, momentum, own_start):
    rows, kinds, heads, size = momentum.shape
    width = keep.shape[1]

    def kernel(keep_ref, got_ref, mom_ref, start_ref, next_ref, share_ref):
        for head in range(heads):
            for kind in range(kinds):
                low = (head * kinds + kind) * size
                cols = slice(low, low + size)
                moment = 0.9 * mom_ref[:, kind, head, :] + (
                    keep_ref[:, cols] + got_ref[:, cols].astype(F32)
                )
                next_ref[:, kind, head, :] = moment
                start = start_ref[:, kind, head, :]
                moved = start - moment
                factor = jnp.sqrt(jnp.sum(start * start, axis=-1, keepdims=True)) / jnp.sqrt(
                    jnp.sum(moved * moved, axis=-1, keepdims=True) + 1e-06
                )
                share_ref[:, cols] = (moved * factor).astype(BF16)

    whole = pl.BlockSpec(memory_space=pltpu.VMEM)
    return pl.pallas_call(
        kernel,
        in_specs=[whole] * 4,
        out_specs=[whole, whole],
        out_shape=[
            jax.ShapeDtypeStruct(momentum.shape, F32),
            jax.ShapeDtypeStruct((rows, width), BF16),
        ],
        compiler_params=pltpu.CompilerParams(vmem_limit_bytes=4 * MIB),
        cost_estimate=cost(8 * rows * width, 20 * rows * width),
        name="update_rows",
    )(keep, received, momentum, own_start)


def project_and_attend(window_ends, arrived, project_weight, heads, first, count):
    tok_dev, width = arrived.shape
    size = width // heads
    windows = window_ends.shape[0]
    tile = 256
    scale = 1.0 / math.sqrt(size)

    def kernel(ends_ref, x_ref, wq_ref, wk_ref, wv_ref, unit_ref, att_ref):
        x = x_ref[...]
        queries = dot(x, wq_ref[...]).astype(BF16)
        keys = dot(x, wk_ref[...]).astype(BF16)
        values = dot(x, wv_ref[...]).astype(BF16)
        wide = queries.astype(F32)
        unit_ref[...] = (
            wide * lax.rsqrt(jnp.mean(wide * wide, axis=-1, keepdims=True) + 1e-06)
        ).astype(BF16)
        key_place = lax.broadcasted_iota(jnp.int32, (1, tok_dev), 1)
        key_window = jnp.zeros((1, tok_dev), jnp.int32)
        for w in range(windows):
            key_window += (key_place >= ends_ref[w]).astype(jnp.int32)
        for start in range(0, tok_dev, tile):
            place = lax.broadcasted_iota(jnp.int32, (tile, 1), 0) + start
            window = jnp.zeros((tile, 1), jnp.int32)
            for w in range(windows):
                window += (place >= ends_ref[w]).astype(jnp.int32)
            scores = dot_nt(queries[start : start + tile], keys) * scale
            scores = jnp.where(window == key_window, scores, -1e30)
            highest = jnp.max(scores, axis=-1, keepdims=True)
            expo = jnp.exp(scores - highest)
            total = jnp.sum(expo, axis=-1, keepdims=True)
            att_ref[start : start + tile, :] = dot(expo.astype(BF16), values) / total

    return pl.pallas_call(
        kernel,
        grid_spec=pltpu.PrefetchScalarGridSpec(
            num_scalar_prefetch=1,
            grid=(count,),
            in_specs=[
                pl.BlockSpec((tok_dev, width), lambda h, e: (0, 0)),
                pl.BlockSpec((width, size), lambda h, e: (0, first + h)),
                pl.BlockSpec((width, size), lambda h, e: (0, heads + first + h)),
                pl.BlockSpec((width, size), lambda h, e: (0, 2 * heads + first + h)),
            ],
            out_specs=[
                pl.BlockSpec((tok_dev, size), lambda h, e: (0, h)),
                pl.BlockSpec((tok_dev, size), lambda h, e: (0, h)),
            ],
        ),
        out_shape=[
            jax.ShapeDtypeStruct((tok_dev, count * size), BF16),
            jax.ShapeDtypeStruct((tok_dev, count * size), F32),
        ],
        compiler_params=params(50),
        cost_estimate=cost(
            2 * tok_dev * count * size * (3 * width + 2 * tok_dev),
            2 * tok_dev * width + 6 * tok_dev * count * size + 6 * width * count * size,
            count * tok_dev * tok_dev,
        ),
        name="project_and_attend",
    )(window_ends, arrived, project_weight, project_weight, project_weight)


def apply_fast(position, gathered, units, attends, norm_gain, output_weight, shards):
    tok_dev = units[0].shape[0]
    width = output_weight.shape[0]
    heads, size = norm_gain.shape
    slab = size // shards
    stages = shards.bit_length() - 1
    tile = 256
    parts = len(gathered)
    part_rows = size // parts
    pieces_of = len(units)
    where = []
    for piece, unit in enumerate(units):
        where += [(piece, low) for low in range(0, unit.shape[1], size)]

    def kernel(pos_ref, *refs):
        part_refs = refs[:parts]
        unit_refs = refs[parts : parts + pieces_of]
        att_refs = refs[parts + pieces_of : parts + 2 * pieces_of]
        gain_ref, ow_ref, mix_ref, wide_ref, fast_ref = refs[parts + 2 * pieces_of :]

        @pl.when(pl.program_id(0) == 0)
        def _():
            for place in range(shards):
                owner = pos_ref[0] ^ bit_reverse(place, stages)
                low = (place * slab) % part_rows
                rows = part_refs[place * slab // part_rows][low : low + slab, :]
                wide_ref[pl.ds(pl.multiple_of(owner * slab, slab), slab), :] = rows.astype(F32)
            fast_ref[...] = wide_ref[...].astype(BF16)

        pieces = []
        for head in range(heads):
            low = head * 3 * size
            piece, col = where[head]
            cols = slice(col, col + size)
            query = unit_refs[piece][:, cols]
            gate = dot(query, fast_ref[:, low : low + size])
            up = dot(query, fast_ref[:, low + size : low + 2 * size])
            hidden = (gate * jax.nn.sigmoid(gate) * up).astype(BF16)
            out = dot_nt(hidden, fast_ref[:, low + 2 * size : low + 3 * size])
            out = out * lax.rsqrt(jnp.mean(out * out, axis=-1, keepdims=True) + 1e-06)
            normed = (out * gain_ref[head : head + 1, :]).astype(BF16).astype(F32)
            pieces.append((normed + att_refs[piece][:, cols]).astype(BF16))
        combined = jnp.concatenate(pieces, axis=1)
        mix_ref[...] = dot(combined, ow_ref[...]).astype(BF16)

    return pl.pallas_call(
        kernel,
        grid_spec=pltpu.PrefetchScalarGridSpec(
            num_scalar_prefetch=1,
            grid=(tok_dev // tile,),
            in_specs=[pl.BlockSpec((part_rows, 3 * width), lambda i, p: (0, 0))] * parts
            + [pl.BlockSpec((tile, unit.shape[1]), lambda i, p: (i, 0)) for unit in units] * 2
            + [
                pl.BlockSpec((heads, size), lambda i, p: (0, 0)),
                pl.BlockSpec((width, width), lambda i, p: (0, 0)),
            ],
            out_specs=pl.BlockSpec((tile, width), lambda i, p: (i, 0)),
            scratch_shapes=[
                pltpu.VMEM((size, 3 * width), F32),
                pltpu.VMEM((size, 3 * width), BF16),
            ],
        ),
        out_shape=jax.ShapeDtypeStruct((tok_dev, width), BF16),
        compiler_params=params(20),
        cost_estimate=cost(
            2 * tok_dev * width * (width + 3 * size),
            8 * tok_dev * width + 2 * width * width + 6 * size * width,
            tok_dev * width,
        ),
        name="apply_fast",
    )(position, *gathered, *units, *attends, norm_gain, output_weight)


def body(
    activations,
    view_id,
    window_lengths,
    project_weight,
    rate_weight,
    fast_start,
    momentum,
    norm_gain,
    output_weight,
):
    tok_dev, width = activations.shape
    shards = lax.axis_size("tok")
    index = lax.axis_index("tok")
    position = index.reshape(1).astype(jnp.int32)
    heads = rate_weight.shape[1]
    size = width // heads
    slab = size // shards

    def swap(array, bit):
        return lax.ppermute(array, "tok", [(i, i ^ bit) for i in range(shards)])

    sent = group_by_view(view_id, activations, shards)
    arrived = lax.all_to_all(
        sent.reshape(shards, tok_dev // shards, width), "tok", split_axis=0, concat_axis=0, tiled=True
    ).reshape(tok_dev, width)
    ends = jnp.cumsum(window_lengths[0])
    own_start = lax.dynamic_slice_in_dim(fast_start, index * slab, slab, 0)

    keep, send = fast_gradient(
        position, after(activations, sent), project_weight, rate_weight, fast_start, shards
    )
    bit = 1
    while bit < shards:
        received = swap(send, bit)
        bit *= 2
        if bit < shards:
            keep, send = add_and_halve(keep, received)
    momentum_next, block = update_rows(keep, received, momentum, own_start)

    stages = shards.bit_length() - 1
    units, attends = [], []
    bit = shards // 2
    done = 0
    for stage in range(stages - 1):
        last = stage == stages - 2
        count = heads - done if last else min(1, heads - done)
        if count:
            unit, attended = project_and_attend(
                ends, after(arrived, block), project_weight, heads, done, count
            )
            units.append(unit)
            attends.append(attended)
            done += count
        other = swap(block, bit)
        if not last:
            block = join(block, after(other, attends[-1]))
            bit //= 2
    gathered = [block, other, swap(block, 1), swap(after(other, attends[-1]), 1)]
    mixed = apply_fast(position, gathered, units, attends, norm_gain, output_weight, shards)
    return (mixed[None], momentum_next)


def solution(mesh):
    in_specs = (
        P(("group", "tok"), None),
        P(("group", "tok")),
        P(("group", "tok"), None),
        P(),
        P(),
        P(),
        P(("group", "tok"), None, None, None),
        P(),
        P(),
    )
    out_specs = (P(("group", "tok"), None, None), P(("group", "tok"), None, None, None))
    return jax.shard_map(body, mesh=mesh, in_specs=in_specs, out_specs=out_specs, check_vma=False)
```

```python
import math

import jax
import jax.numpy as jnp
from jax import lax
from jax.experimental import pallas as pl
from jax.experimental.pallas import tpu as pltpu
from jax.sharding import PartitionSpec as P

F32 = jnp.float32
BF16 = jnp.bfloat16
MIB = 1024 * 1024


def dot(a, b):
    return jnp.dot(a, b, preferred_element_type=F32)


def dot_tn(a, b):
    return lax.dot_general(a, b, (((0,), (0,)), ((), ())), preferred_element_type=F32)


def dot_nt(a, b):
    return lax.dot_general(a, b, (((1,), (1,)), ((), ())), preferred_element_type=F32)


def offset_of(place, order):
    out = 0
    for step, bit in enumerate(order):
        if (place >> (len(order) - 1 - step)) & 1:
            out |= bit
    return out


def params(mebibytes):
    return pltpu.CompilerParams(
        dimension_semantics=("arbitrary",), vmem_limit_bytes=mebibytes * MIB
    )


def after(array, *others):
    return lax.optimization_barrier((array, *others))[0]


def cost(flops, nbytes, transcendentals=0):
    return pl.CostEstimate(
        flops=int(flops), bytes_accessed=int(nbytes), transcendentals=int(transcendentals)
    )


def group_by_view(view_id, activations, shards):
    tok_dev, width = activations.shape
    per_view = tok_dev // shards
    chunk = 256
    tile = 256

    def kernel(view_ref, act_ref, out_ref, slot_ref):
        @pl.when(pl.program_id(0) == 0)
        def _():
            rows = lax.broadcasted_iota(jnp.int32, (chunk, chunk), 0)
            cols = lax.broadcasted_iota(jnp.int32, (chunk, chunk), 1)
            upper = jnp.where(rows < cols, 1.0, 0.0).astype(BF16)
            views = lax.broadcasted_iota(jnp.int32, (shards, chunk), 0)
            before = jnp.zeros((shards, 1), F32)
            for start in range(0, tok_dev, chunk):
                member = views == view_ref[:, start : start + chunk]
                hot = jnp.where(member, 1.0, 0.0)
                rank = dot(hot.astype(BF16), upper) + before
                slot = jnp.where(member, rank + (views * per_view).astype(F32), 0.0)
                slot_ref[:, start : start + chunk] = jnp.sum(slot, axis=0, keepdims=True).astype(
                    jnp.int32
                )
                before = before + jnp.sum(hot, axis=1, keepdims=True)

        target = lax.broadcasted_iota(jnp.int32, (tile, tok_dev), 0) + pl.program_id(0) * tile
        pick = jnp.where(target == slot_ref[...], 1.0, 0.0).astype(BF16)
        out_ref[...] = dot(pick, act_ref[...]).astype(BF16)

    return pl.pallas_call(
        kernel,
        grid=(tok_dev // tile,),
        in_specs=[
            pl.BlockSpec((1, tok_dev), lambda i: (0, 0)),
            pl.BlockSpec((tok_dev, width), lambda i: (0, 0)),
        ],
        out_specs=pl.BlockSpec((tile, width), lambda i: (i, 0)),
        out_shape=jax.ShapeDtypeStruct((tok_dev, width), BF16),
        scratch_shapes=[pltpu.VMEM((1, tok_dev), jnp.int32)],
        compiler_params=params(60),
        cost_estimate=cost(2 * tok_dev * tok_dev * width, 4 * tok_dev * width),
        name="group_by_view",
    )(view_id.reshape(1, tok_dev), activations)


def fast_gradient(
    position, activations, project_weight, rate_weight, fast_start, first, count, order
):
    tok_dev, width = activations.shape
    heads = rate_weight.shape[1]
    kinds = fast_start.shape[1]
    size = width // heads
    shards = 1 << len(order)
    slab = size // shards
    tile = 256
    scale = 0.1 / math.sqrt(tok_dev * shards)
    half = size // 2

    def kernel(pos_ref, act_ref, wk_ref, wv_ref, rate_w_ref, fast_ref, keep_ref, send_ref,
               rate_ref, key_ref, out_ref, hid_ref, gate_ref, grad_ref, start_ref, sems):
        step = pl.program_id(0)
        head = first + step
        slot = step % 2

        def fetch(which, place):
            return [
                pltpu.make_async_copy(
                    fast_ref.at[:, kind, which, :], start_ref.at[place, kind], sems.at[place, kind]
                )
                for kind in range(kinds)
            ]

        @pl.when(step == 0)
        def _():
            for copy in fetch(first, 0):
                copy.start()
            raw = dot_nt(act_ref[...], rate_w_ref[...])
            rate_ref[...] = (jnp.maximum(raw, 0.0) + jnp.log1p(jnp.exp(-jnp.abs(raw)))) * scale

        @pl.when(step + 1 < count)
        def _():
            for copy in fetch(head + 1, 1 - slot):
                copy.start()

        for copy in fetch(head, slot):
            copy.wait()
        w_gate, w_up, w_down = [start_ref[slot, kind].astype(BF16) for kind in range(kinds)]
        for start in range(0, tok_dev, tile):
            rows = slice(start, start + tile)
            act = act_ref[rows, :]
            keys = dot(act, wk_ref[...]).astype(BF16).astype(F32)
            values = dot(act, wv_ref[...]).astype(BF16).astype(F32)
            key_unit = (
                keys * lax.rsqrt(jnp.mean(keys * keys, axis=-1, keepdims=True) + 1e-06)
            ).astype(BF16)
            lanes = lax.broadcasted_iota(jnp.int32, (tile, heads), 1)
            rate = jnp.sum(
                jnp.where(lanes == head, rate_ref[rows, :], 0.0), axis=1, keepdims=True
            )
            back_out = (-rate * values).astype(BF16)
            pre_gate = dot(key_unit, w_gate)
            pre_up = dot(key_unit, w_up)
            back_hidden = dot(back_out, w_down)
            sig = jax.nn.sigmoid(pre_gate)
            act_gate = pre_gate * sig
            key_ref[rows, :] = key_unit
            out_ref[rows, :] = back_out
            hid_ref[rows, :] = (act_gate * pre_up).astype(BF16)
            gate_ref[rows, 0:size] = (
                back_hidden * pre_up * sig * (1.0 + pre_gate * (1.0 - sig))
            ).astype(BF16)
            gate_ref[rows, size : 2 * size] = (back_hidden * act_gate).astype(BF16)
        grad_ref[:, 0 : 2 * size] = dot_tn(key_ref[...], gate_ref[...])
        grad_ref[:, 2 * size : 3 * size] = dot_tn(out_ref[...], hid_ref[...])
        for place in range(shards):
            owner = pos_ref[0] ^ offset_of(place, order)
            rows = grad_ref[pl.ds(pl.multiple_of(owner * slab, slab), slab), :]
            if place < shards // 2:
                keep_ref[place * slab : (place + 1) * slab, :] = rows
            else:
                low = place * slab - half
                send_ref[low : low + slab, :] = rows.astype(BF16)

    return pl.pallas_call(
        kernel,
        grid_spec=pltpu.PrefetchScalarGridSpec(
            num_scalar_prefetch=1,
            grid=(count,),
            in_specs=[
                pl.BlockSpec((tok_dev, width), lambda h, p: (0, 0)),
                pl.BlockSpec((width, size), lambda h, p: (0, heads + first + h)),
                pl.BlockSpec((width, size), lambda h, p: (0, 2 * heads + first + h)),
                pl.BlockSpec((heads, width), lambda h, p: (0, 0)),
                pl.BlockSpec(memory_space=pl.ANY),
            ],
            out_specs=[
                pl.BlockSpec((half, 3 * size), lambda h, p: (0, h)),
                pl.BlockSpec((half, 3 * size), lambda h, p: (0, h)),
            ],
            scratch_shapes=[
                pltpu.VMEM((tok_dev, heads), F32),
                pltpu.VMEM((tok_dev, size), BF16),
                pltpu.VMEM((tok_dev, size), BF16),
                pltpu.VMEM((tok_dev, size), BF16),
                pltpu.VMEM((tok_dev, 2 * size), BF16),
                pltpu.VMEM((size, 3 * size), F32),
                pltpu.VMEM((2, kinds, size, size), F32),
                pltpu.SemaphoreType.DMA((2, kinds)),
            ],
        ),
        out_shape=[
            jax.ShapeDtypeStruct((half, 3 * size * count), F32),
            jax.ShapeDtypeStruct((half, 3 * size * count), BF16),
        ],
        compiler_params=params(60),
        cost_estimate=cost(
            2 * tok_dev * size * count * (2 * width + 6 * size),
            2 * tok_dev * width + 4 * width * size * count + 20 * size * size * count,
            4 * tok_dev * size * count,
        ),
        name="fast_gradient",
    )(position, activations, project_weight, project_weight, rate_weight.T, fast_start)


def add_and_halve(keep, received):
    rows, width = keep.shape
    half = rows // 2

    def kernel(keep_ref, got_ref, stay_ref, go_ref):
        stay_ref[...] = keep_ref[:half, :] + got_ref[:half, :].astype(F32)
        go_ref[...] = (keep_ref[half:, :] + got_ref[half:, :].astype(F32)).astype(BF16)

    whole = pl.BlockSpec(memory_space=pltpu.VMEM)
    return pl.pallas_call(
        kernel,
        in_specs=[whole, whole],
        out_specs=[whole, whole],
        out_shape=[
            jax.ShapeDtypeStruct((half, width), F32),
            jax.ShapeDtypeStruct((half, width), BF16),
        ],
        compiler_params=pltpu.CompilerParams(vmem_limit_bytes=6 * MIB),
        cost_estimate=cost(rows * width, 9 * rows * width),
        name="add_and_halve",
    )(keep, received)


def update_rows(keeps, receiveds, momentum, own_start):
    rows, kinds, heads, size = momentum.shape
    width = heads * kinds * size
    streams = len(keeps)
    stream_heads = heads // streams

    def kernel(*refs):
        keep_refs = refs[:streams]
        got_refs = refs[streams : 2 * streams]
        mom_ref, start_ref, next_ref, share_ref = refs[2 * streams :]
        for head in range(heads):
            keep_ref = keep_refs[head // stream_heads]
            got_ref = got_refs[head // stream_heads]
            for kind in range(kinds):
                low = ((head % stream_heads) * kinds + kind) * size
                cols = slice(low, low + size)
                moment = 0.9 * mom_ref[:, kind, head, :] + (
                    keep_ref[:, cols] + got_ref[:, cols].astype(F32)
                )
                next_ref[:, kind, head, :] = moment
                start = start_ref[:, kind, head, :]
                moved = start - moment
                factor = jnp.sqrt(jnp.sum(start * start, axis=-1, keepdims=True)) / jnp.sqrt(
                    jnp.sum(moved * moved, axis=-1, keepdims=True) + 1e-06
                )
                low = (head * kinds + kind) * size
                share_ref[:, low : low + size] = (moved * factor).astype(BF16)

    whole = pl.BlockSpec(memory_space=pltpu.VMEM)
    return pl.pallas_call(
        kernel,
        in_specs=[whole] * (2 * streams + 2),
        out_specs=[whole, whole],
        out_shape=[
            jax.ShapeDtypeStruct(momentum.shape, F32),
            jax.ShapeDtypeStruct((rows, width), BF16),
        ],
        compiler_params=pltpu.CompilerParams(vmem_limit_bytes=4 * MIB),
        cost_estimate=cost(8 * rows * width, 20 * rows * width),
        name="update_rows",
    )(*keeps, *receiveds, momentum, own_start)


def project_and_attend(window_ends, arrived, project_weight, heads, first, count):
    tok_dev, width = arrived.shape
    size = width // heads
    windows = window_ends.shape[0]
    tile = 256
    scale = 1.0 / math.sqrt(size)

    def kernel(ends_ref, x_ref, wq_ref, wk_ref, wv_ref, unit_ref, att_ref):
        x = x_ref[...]
        queries = dot(x, wq_ref[...]).astype(BF16)
        keys = dot(x, wk_ref[...]).astype(BF16)
        values = dot(x, wv_ref[...]).astype(BF16)
        wide = queries.astype(F32)
        unit_ref[...] = (
            wide * lax.rsqrt(jnp.mean(wide * wide, axis=-1, keepdims=True) + 1e-06)
        ).astype(BF16)
        key_place = lax.broadcasted_iota(jnp.int32, (1, tok_dev), 1)
        key_window = jnp.zeros((1, tok_dev), jnp.int32)
        for w in range(windows):
            key_window += (key_place >= ends_ref[w]).astype(jnp.int32)
        for start in range(0, tok_dev, tile):
            place = lax.broadcasted_iota(jnp.int32, (tile, 1), 0) + start
            window = jnp.zeros((tile, 1), jnp.int32)
            for w in range(windows):
                window += (place >= ends_ref[w]).astype(jnp.int32)
            scores = dot_nt(queries[start : start + tile], keys) * scale
            scores = jnp.where(window == key_window, scores, -1e30)
            highest = jnp.max(scores, axis=-1, keepdims=True)
            expo = jnp.exp(scores - highest)
            total = jnp.sum(expo, axis=-1, keepdims=True)
            att_ref[start : start + tile, :] = dot(expo.astype(BF16), values) / total

    return pl.pallas_call(
        kernel,
        grid_spec=pltpu.PrefetchScalarGridSpec(
            num_scalar_prefetch=1,
            grid=(count,),
            in_specs=[
                pl.BlockSpec((tok_dev, width), lambda h, e: (0, 0)),
                pl.BlockSpec((width, size), lambda h, e: (0, first + h)),
                pl.BlockSpec((width, size), lambda h, e: (0, heads + first + h)),
                pl.BlockSpec((width, size), lambda h, e: (0, 2 * heads + first + h)),
            ],
            out_specs=[
                pl.BlockSpec((tok_dev, size), lambda h, e: (0, h)),
                pl.BlockSpec((tok_dev, size), lambda h, e: (0, h)),
            ],
        ),
        out_shape=[
            jax.ShapeDtypeStruct((tok_dev, count * size), BF16),
            jax.ShapeDtypeStruct((tok_dev, count * size), F32),
        ],
        compiler_params=params(50),
        cost_estimate=cost(
            2 * tok_dev * count * size * (3 * width + 2 * tok_dev),
            2 * tok_dev * width + 6 * tok_dev * count * size + 6 * width * count * size,
            count * tok_dev * tok_dev,
        ),
        name="project_and_attend",
    )(window_ends, arrived, project_weight, project_weight, project_weight)


def apply_fast(position, gathered, units, attends, norm_gain, output_weight, shards):
    tok_dev = units[0].shape[0]
    width = output_weight.shape[0]
    heads, size = norm_gain.shape
    slab = size // shards
    tile = 256
    parts = len(gathered)
    part_rows = size // parts
    pieces_of = len(units)
    where = []
    for piece, unit in enumerate(units):
        where += [(piece, low) for low in range(0, unit.shape[1], size)]

    def kernel(pos_ref, *refs):
        part_refs = refs[:parts]
        unit_refs = refs[parts : parts + pieces_of]
        att_refs = refs[parts + pieces_of : parts + 2 * pieces_of]
        gain_ref, ow_ref, mix_ref, wide_ref, fast_ref = refs[parts + 2 * pieces_of :]

        @pl.when(pl.program_id(0) == 0)
        def _():
            core = pos_ref[0] % parts
            for part in range(parts):
                for place in range(shards // parts):
                    owner = place * parts + (core ^ part)
                    rows = part_refs[part][place * slab : (place + 1) * slab, :]
                    wide_ref[pl.ds(pl.multiple_of(owner * slab, slab), slab), :] = rows.astype(F32)
            fast_ref[...] = wide_ref[...].astype(BF16)

        pieces = []
        for head in range(heads):
            low = head * 3 * size
            piece, col = where[head]
            cols = slice(col, col + size)
            query = unit_refs[piece][:, cols]
            gate = dot(query, fast_ref[:, low : low + size])
            up = dot(query, fast_ref[:, low + size : low + 2 * size])
            hidden = (gate * jax.nn.sigmoid(gate) * up).astype(BF16)
            out = dot_nt(hidden, fast_ref[:, low + 2 * size : low + 3 * size])
            out = out * lax.rsqrt(jnp.mean(out * out, axis=-1, keepdims=True) + 1e-06)
            normed = (out * gain_ref[head : head + 1, :]).astype(BF16).astype(F32)
            pieces.append((normed + att_refs[piece][:, cols]).astype(BF16))
        combined = jnp.concatenate(pieces, axis=1)
        mix_ref[...] = dot(combined, ow_ref[...]).astype(BF16)

    return pl.pallas_call(
        kernel,
        grid_spec=pltpu.PrefetchScalarGridSpec(
            num_scalar_prefetch=1,
            grid=(tok_dev // tile,),
            in_specs=[pl.BlockSpec((part_rows, 3 * width), lambda i, p: (0, 0))] * parts
            + [pl.BlockSpec((tile, unit.shape[1]), lambda i, p: (i, 0)) for unit in units] * 2
            + [
                pl.BlockSpec((heads, size), lambda i, p: (0, 0)),
                pl.BlockSpec((width, width), lambda i, p: (0, 0)),
            ],
            out_specs=pl.BlockSpec((tile, width), lambda i, p: (i, 0)),
            scratch_shapes=[
                pltpu.VMEM((size, 3 * width), F32),
                pltpu.VMEM((size, 3 * width), BF16),
            ],
        ),
        out_shape=jax.ShapeDtypeStruct((tok_dev, width), BF16),
        compiler_params=params(20),
        cost_estimate=cost(
            2 * tok_dev * width * (width + 3 * size),
            8 * tok_dev * width + 2 * width * width + 6 * size * width,
            tok_dev * width,
        ),
        name="apply_fast",
    )(position, *gathered, *units, *attends, norm_gain, output_weight)


def body(
    activations,
    view_id,
    window_lengths,
    project_weight,
    rate_weight,
    fast_start,
    momentum,
    norm_gain,
    output_weight,
):
    tok_dev, width = activations.shape
    shards = lax.axis_size("tok")
    index = lax.axis_index("tok")
    position = index.reshape(1).astype(jnp.int32)
    heads = rate_weight.shape[1]
    size = width // heads
    slab = size // shards

    def swap(array, bit):
        return lax.ppermute(array, "tok", [(i, i ^ bit) for i in range(shards)])

    sent = group_by_view(view_id, activations, shards)
    arrived = lax.all_to_all(
        sent.reshape(shards, tok_dev // shards, width), "tok", split_axis=0, concat_axis=0, tiled=True
    ).reshape(tok_dev, width)
    ends = jnp.cumsum(window_lengths[0])
    own_start = lax.dynamic_slice_in_dim(fast_start, index * slab, slab, 0)

    bits = [1 << step for step in range(shards.bit_length() - 1)]
    orders = [bits, bits[:1] + bits[2:] + bits[1:2]]
    count = heads // len(orders)
    keeps, receiveds = [], []
    for stream, order in enumerate(orders):
        keep, send = fast_gradient(
            position, after(activations, sent), project_weight, rate_weight, fast_start,
            stream * count, count, order,
        )
        for step, bit in enumerate(order):
            received = swap(send, bit)
            if step + 1 < len(order):
                keep, send = add_and_halve(keep, received)
        keeps.append(keep)
        receiveds.append(received)
    momentum_next, share = update_rows(keeps, receiveds, momentum, own_start)

    cores = [[i for i in range(shards) if i % 2 == core] for core in range(2)]
    block = lax.all_to_all(
        jnp.broadcast_to(after(share, arrived)[None], (shards // 2, *share.shape)), "tok",
        split_axis=0, concat_axis=0, tiled=True, axis_index_groups=cores,
    ).reshape(size // 2, 3 * width)
    unit, attended = project_and_attend(ends, after(arrived, share), project_weight, heads, 0, heads)
    units, attends = [unit], [attended]
    gathered = [block, swap(after(block, attended), 1)]
    mixed = apply_fast(position, gathered, units, attends, norm_gain, output_weight, shards)
    return (mixed[None], momentum_next)


def solution(mesh):
    in_specs = (
        P(("group", "tok"), None),
        P(("group", "tok")),
        P(("group", "tok"), None),
        P(),
        P(),
        P(),
        P(("group", "tok"), None, None, None),
        P(),
        P(),
    )
    out_specs = (P(("group", "tok"), None, None), P(("group", "tok"), None, None, None))
    return jax.shard_map(body, mesh=mesh, in_specs=in_specs, out_specs=out_specs, check_vma=False)
```

```python
import math

import jax
import jax.numpy as jnp
from jax import lax
from jax.experimental import pallas as pl
from jax.experimental.pallas import tpu as pltpu
from jax.sharding import PartitionSpec as P

F32 = jnp.float32
BF16 = jnp.bfloat16
MIB = 1024 * 1024


def dot(a, b):
    return jnp.dot(a, b, preferred_element_type=F32)


def dot_tn(a, b):
    return lax.dot_general(a, b, (((0,), (0,)), ((), ())), preferred_element_type=F32)


def dot_nt(a, b):
    return lax.dot_general(a, b, (((1,), (1,)), ((), ())), preferred_element_type=F32)


def bit_reverse(value, width):
    out = 0
    for bit in range(width):
        out |= ((value >> bit) & 1) << (width - 1 - bit)
    return out


def params(mebibytes):
    return pltpu.CompilerParams(
        dimension_semantics=("arbitrary",), vmem_limit_bytes=mebibytes * MIB
    )


def after(array, *others):
    return lax.optimization_barrier((array, *others))[0]


def cost(flops, nbytes, transcendentals=0):
    return pl.CostEstimate(
        flops=int(flops), bytes_accessed=int(nbytes), transcendentals=int(transcendentals)
    )


def group_by_view(view_id, activations, shards):
    tok_dev, width = activations.shape
    per_view = tok_dev // shards
    chunk = 256
    tile = 1024

    def kernel(view_ref, act_ref, out_ref, slot_ref):
        @pl.when(pl.program_id(0) == 0)
        def _():
            rows = lax.broadcasted_iota(jnp.int32, (chunk, chunk), 0)
            cols = lax.broadcasted_iota(jnp.int32, (chunk, chunk), 1)
            upper = jnp.where(rows < cols, 1.0, 0.0).astype(BF16)
            views = lax.broadcasted_iota(jnp.int32, (shards, chunk), 0)
            before = jnp.zeros((shards, 1), F32)
            for start in range(0, tok_dev, chunk):
                member = views == view_ref[:, start : start + chunk]
                hot = jnp.where(member, 1.0, 0.0)
                rank = dot(hot.astype(BF16), upper) + before
                slot = jnp.where(member, rank + (views * per_view).astype(F32), 0.0)
                slot_ref[:, start : start + chunk] = jnp.sum(slot, axis=0, keepdims=True).astype(
                    jnp.int32
                )
                before = before + jnp.sum(hot, axis=1, keepdims=True)

        target = lax.broadcasted_iota(jnp.int32, (tile, tok_dev), 0) + pl.program_id(0) * tile
        pick = jnp.where(target == slot_ref[...], 1.0, 0.0).astype(BF16)
        out_ref[...] = dot(pick, act_ref[...]).astype(BF16)

    return pl.pallas_call(
        kernel,
        grid=(tok_dev // tile,),
        in_specs=[
            pl.BlockSpec((1, tok_dev), lambda i: (0, 0)),
            pl.BlockSpec((tok_dev, width), lambda i: (0, 0)),
        ],
        out_specs=pl.BlockSpec((tile, width), lambda i: (i, 0)),
        out_shape=jax.ShapeDtypeStruct((tok_dev, width), BF16),
        scratch_shapes=[pltpu.VMEM((1, tok_dev), jnp.int32)],
        compiler_params=params(60),
        cost_estimate=cost(2 * tok_dev * tok_dev * width, 4 * tok_dev * width),
        name="group_by_view",
    )(view_id.reshape(1, tok_dev), activations)


def fast_gradient(position, activations, project_weight, rate_weight, fast_start, shards):
    tok_dev, width = activations.shape
    heads = rate_weight.shape[1]
    kinds = fast_start.shape[1]
    size = width // heads
    slab = size // shards
    stages = shards.bit_length() - 1
    tile = 1024
    scale = 0.1 / math.sqrt(tok_dev * shards)
    half = size // 2

    def kernel(pos_ref, act_ref, wk_ref, wv_ref, rate_w_ref, fast_ref, keep_ref, send_ref,
               rate_ref, key_ref, out_ref, hid_ref, gate_ref, grad_ref, start_ref, sems):
        head = pl.program_id(0)
        slot = head % 2

        def fetch(which, place):
            return [
                pltpu.make_async_copy(
                    fast_ref.at[:, kind, which, :], start_ref.at[place, kind], sems.at[place, kind]
                )
                for kind in range(kinds)
            ]

        @pl.when(head == 0)
        def _():
            for copy in fetch(0, 0):
                copy.start()
            raw = dot_nt(act_ref[...], rate_w_ref[...])
            rate_ref[...] = (jnp.maximum(raw, 0.0) + jnp.log1p(jnp.exp(-jnp.abs(raw)))) * scale

        @pl.when(head + 1 < heads)
        def _():
            for copy in fetch(head + 1, 1 - slot):
                copy.start()

        for copy in fetch(head, slot):
            copy.wait()
        w_gate, w_up, w_down = [start_ref[slot, kind].astype(BF16) for kind in range(kinds)]
        for start in range(0, tok_dev, tile):
            rows = slice(start, start + tile)
            act = act_ref[rows, :]
            keys = dot(act, wk_ref[...]).astype(BF16).astype(F32)
            values = dot(act, wv_ref[...]).astype(BF16).astype(F32)
            key_unit = (
                keys * lax.rsqrt(jnp.mean(keys * keys, axis=-1, keepdims=True) + 1e-06)
            ).astype(BF16)
            lanes = lax.broadcasted_iota(jnp.int32, (tile, heads), 1)
            rate = jnp.sum(
                jnp.where(lanes == head, rate_ref[rows, :], 0.0), axis=1, keepdims=True
            )
            back_out = (-rate * values).astype(BF16)
            pre_gate = dot(key_unit, w_gate)
            pre_up = dot(key_unit, w_up)
            back_hidden = dot(back_out, w_down)
            sig = jax.nn.sigmoid(pre_gate)
            act_gate = pre_gate * sig
            key_ref[rows, :] = key_unit
            out_ref[rows, :] = back_out
            hid_ref[rows, :] = (act_gate * pre_up).astype(BF16)
            gate_ref[rows, 0:size] = (
                back_hidden * pre_up * sig * (1.0 + pre_gate * (1.0 - sig))
            ).astype(BF16)
            gate_ref[rows, size : 2 * size] = (back_hidden * act_gate).astype(BF16)
        grad_ref[:, 0 : 2 * size] = dot_tn(key_ref[...], gate_ref[...])
        grad_ref[:, 2 * size : 3 * size] = dot_tn(out_ref[...], hid_ref[...])
        for place in range(shards):
            owner = pos_ref[0] ^ bit_reverse(place, stages)
            rows = grad_ref[pl.ds(pl.multiple_of(owner * slab, slab), slab), :]
            if place < shards // 2:
                keep_ref[place * slab : (place + 1) * slab, :] = rows
            else:
                low = place * slab - half
                send_ref[low : low + slab, :] = rows.astype(BF16)

    return pl.pallas_call(
        kernel,
        grid_spec=pltpu.PrefetchScalarGridSpec(
            num_scalar_prefetch=1,
            grid=(heads,),
            in_specs=[
                pl.BlockSpec((tok_dev, width), lambda h, p: (0, 0)),
                pl.BlockSpec((width, size), lambda h, p: (0, heads + h)),
                pl.BlockSpec((width, size), lambda h, p: (0, 2 * heads + h)),
                pl.BlockSpec((heads, width), lambda h, p: (0, 0)),
                pl.BlockSpec(memory_space=pl.ANY),
            ],
            out_specs=[
                pl.BlockSpec((half, 3 * size), lambda h, p: (0, h)),
                pl.BlockSpec((half, 3 * size), lambda h, p: (0, h)),
            ],
            scratch_shapes=[
                pltpu.VMEM((tok_dev, heads), F32),
                pltpu.VMEM((tok_dev, size), BF16),
                pltpu.VMEM((tok_dev, size), BF16),
                pltpu.VMEM((tok_dev, size), BF16),
                pltpu.VMEM((tok_dev, 2 * size), BF16),
                pltpu.VMEM((size, 3 * size), F32),
                pltpu.VMEM((2, kinds, size, size), F32),
                pltpu.SemaphoreType.DMA((2, kinds)),
            ],
        ),
        out_shape=[
            jax.ShapeDtypeStruct((half, 3 * width), F32),
            jax.ShapeDtypeStruct((half, 3 * width), BF16),
        ],
        compiler_params=params(60),
        cost_estimate=cost(
            2 * tok_dev * width * (2 * width + 6 * size),
            2 * tok_dev * width + 4 * width * width + 6 * size * width + 9 * size * width,
            4 * tok_dev * width,
        ),
        name="fast_gradient",
    )(position, activations, project_weight, project_weight, rate_weight.T, fast_start)


def add_and_halve(keep, received):
    rows, width = keep.shape
    half = rows // 2

    def kernel(keep_ref, got_ref, stay_ref, go_ref):
        stay_ref[...] = keep_ref[:half, :] + got_ref[:half, :].astype(F32)
        go_ref[...] = (keep_ref[half:, :] + got_ref[half:, :].astype(F32)).astype(BF16)

    whole = pl.BlockSpec(memory_space=pltpu.VMEM)
    return pl.pallas_call(
        kernel,
        in_specs=[whole, whole],
        out_specs=[whole, whole],
        out_shape=[
            jax.ShapeDtypeStruct((half, width), F32),
            jax.ShapeDtypeStruct((half, width), BF16),
        ],
        compiler_params=pltpu.CompilerParams(vmem_limit_bytes=6 * MIB),
        cost_estimate=cost(rows * width, 9 * rows * width),
        name="add_and_halve",
    )(keep, received)


def join(first, second):
    rows, width = first.shape

    def kernel(first_ref, second_ref, out_ref):
        out_ref[:rows, :] = first_ref[...]
        out_ref[rows:, :] = second_ref[...]

    whole = pl.BlockSpec(memory_space=pltpu.VMEM)
    return pl.pallas_call(
        kernel,
        in_specs=[whole, whole],
        out_specs=whole,
        out_shape=jax.ShapeDtypeStruct((2 * rows, width), BF16),
        compiler_params=pltpu.CompilerParams(vmem_limit_bytes=4 * MIB),
        cost_estimate=cost(0, 8 * rows * width),
        name="join",
    )(first, second)


def update_rows(keep, received, momentum, own_start):
    rows, kinds, heads, size = momentum.shape
    width = keep.shape[1]

    def kernel(keep_ref, got_ref, mom_ref, start_ref, next_ref, share_ref):
        for head in range(heads):
            for kind in range(kinds):
                low = (head * kinds + kind) * size
                cols = slice(low, low + size)
                moment = 0.9 * mom_ref[:, kind, head, :] + (
                    keep_ref[:, cols] + got_ref[:, cols].astype(F32)
                )
                next_ref[:, kind, head, :] = moment
                start = start_ref[:, kind, head, :]
                moved = start - moment
                factor = jnp.sqrt(jnp.sum(start * start, axis=-1, keepdims=True)) / jnp.sqrt(
                    jnp.sum(moved * moved, axis=-1, keepdims=True) + 1e-06
                )
                share_ref[:, cols] = (moved * factor).astype(BF16)

    whole = pl.BlockSpec(memory_space=pltpu.VMEM)
    return pl.pallas_call(
        kernel,
        in_specs=[whole] * 4,
        out_specs=[whole, whole],
        out_shape=[
            jax.ShapeDtypeStruct(momentum.shape, F32),
            jax.ShapeDtypeStruct((rows, width), BF16),
        ],
        compiler_params=pltpu.CompilerParams(vmem_limit_bytes=4 * MIB),
        cost_estimate=cost(8 * rows * width, 20 * rows * width),
        name="update_rows",
    )(keep, received, momentum, own_start)


def project_and_attend(window_ends, arrived, project_weight, heads, first, count):
    tok_dev, width = arrived.shape
    size = width // heads
    windows = window_ends.shape[0]
    tile = 512
    scale = 1.0 / math.sqrt(size)

    def kernel(ends_ref, x_ref, wq_ref, wk_ref, wv_ref, unit_ref, att_ref):
        x = x_ref[...]
        queries = dot(x, wq_ref[...]).astype(BF16)
        keys = dot(x, wk_ref[...]).astype(BF16)
        values = dot(x, wv_ref[...]).astype(BF16)
        wide = queries.astype(F32)
        unit_ref[...] = (
            wide * lax.rsqrt(jnp.mean(wide * wide, axis=-1, keepdims=True) + 1e-06)
        ).astype(BF16)
        key_place = lax.broadcasted_iota(jnp.int32, (1, tok_dev), 1)
        key_window = jnp.zeros((1, tok_dev), jnp.int32)
        for w in range(windows):
            key_window += (key_place >= ends_ref[w]).astype(jnp.int32)
        for start in range(0, tok_dev, tile):
            place = lax.broadcasted_iota(jnp.int32, (tile, 1), 0) + start
            window = jnp.zeros((tile, 1), jnp.int32)
            for w in range(windows):
                window += (place >= ends_ref[w]).astype(jnp.int32)
            scores = dot_nt(queries[start : start + tile], keys) * scale
            scores = jnp.where(window == key_window, scores, -1e30)
            highest = jnp.max(scores, axis=-1, keepdims=True)
            expo = jnp.exp(scores - highest)
            total = jnp.sum(expo, axis=-1, keepdims=True)
            att_ref[start : start + tile, :] = dot(expo.astype(BF16), values) / total

    return pl.pallas_call(
        kernel,
        grid_spec=pltpu.PrefetchScalarGridSpec(
            num_scalar_prefetch=1,
            grid=(count,),
            in_specs=[
                pl.BlockSpec((tok_dev, width), lambda h, e: (0, 0)),
                pl.BlockSpec((width, size), lambda h, e: (0, first + h)),
                pl.BlockSpec((width, size), lambda h, e: (0, heads + first + h)),
                pl.BlockSpec((width, size), lambda h, e: (0, 2 * heads + first + h)),
            ],
            out_specs=[
                pl.BlockSpec((tok_dev, size), lambda h, e: (0, h)),
                pl.BlockSpec((tok_dev, size), lambda h, e: (0, h)),
            ],
        ),
        out_shape=[
            jax.ShapeDtypeStruct((tok_dev, count * size), BF16),
            jax.ShapeDtypeStruct((tok_dev, count * size), F32),
        ],
        compiler_params=params(50),
        cost_estimate=cost(
            2 * tok_dev * count * size * (3 * width + 2 * tok_dev),
            2 * tok_dev * width + 6 * tok_dev * count * size + 6 * width * count * size,
            count * tok_dev * tok_dev,
        ),
        name="project_and_attend",
    )(window_ends, arrived, project_weight, project_weight, project_weight)


def apply_fast(position, gathered, units, attends, norm_gain, output_weight, shards):
    tok_dev = units[0].shape[0]
    width = output_weight.shape[0]
    heads, size = norm_gain.shape
    slab = size // shards
    stages = shards.bit_length() - 1
    tile = 1024
    parts = len(gathered)
    part_rows = size // parts
    pieces_of = len(units)
    where = []
    for piece, unit in enumerate(units):
        where += [(piece, low) for low in range(0, unit.shape[1], size)]

    def kernel(pos_ref, *refs):
        part_refs = refs[:parts]
        unit_refs = refs[parts : parts + pieces_of]
        att_refs = refs[parts + pieces_of : parts + 2 * pieces_of]
        gain_ref, ow_ref, mix_ref, wide_ref, fast_ref = refs[parts + 2 * pieces_of :]

        @pl.when(pl.program_id(0) == 0)
        def _():
            for place in range(shards):
                owner = pos_ref[0] ^ bit_reverse(place, stages)
                low = (place * slab) % part_rows
                rows = part_refs[place * slab // part_rows][low : low + slab, :]
                wide_ref[pl.ds(pl.multiple_of(owner * slab, slab), slab), :] = rows.astype(F32)
            fast_ref[...] = wide_ref[...].astype(BF16)

        pieces = []
        for head in range(heads):
            low = head * 3 * size
            piece, col = where[head]
            cols = slice(col, col + size)
            query = unit_refs[piece][:, cols]
            gate = dot(query, fast_ref[:, low : low + size])
            up = dot(query, fast_ref[:, low + size : low + 2 * size])
            hidden = (gate * jax.nn.sigmoid(gate) * up).astype(BF16)
            out = dot_nt(hidden, fast_ref[:, low + 2 * size : low + 3 * size])
            out = out * lax.rsqrt(jnp.mean(out * out, axis=-1, keepdims=True) + 1e-06)
            normed = (out * gain_ref[head : head + 1, :]).astype(BF16).astype(F32)
            pieces.append((normed + att_refs[piece][:, cols]).astype(BF16))
        combined = jnp.concatenate(pieces, axis=1)
        mix_ref[...] = dot(combined, ow_ref[...]).astype(BF16)

    return pl.pallas_call(
        kernel,
        grid_spec=pltpu.PrefetchScalarGridSpec(
            num_scalar_prefetch=1,
            grid=(tok_dev // tile,),
            in_specs=[pl.BlockSpec((part_rows, 3 * width), lambda i, p: (0, 0))] * parts
            + [pl.BlockSpec((tile, unit.shape[1]), lambda i, p: (i, 0)) for unit in units] * 2
            + [
                pl.BlockSpec((heads, size), lambda i, p: (0, 0)),
                pl.BlockSpec((width, width), lambda i, p: (0, 0)),
            ],
            out_specs=pl.BlockSpec((tile, width), lambda i, p: (i, 0)),
            scratch_shapes=[
                pltpu.VMEM((size, 3 * width), F32),
                pltpu.VMEM((size, 3 * width), BF16),
            ],
        ),
        out_shape=jax.ShapeDtypeStruct((tok_dev, width), BF16),
        compiler_params=params(40),
        cost_estimate=cost(
            2 * tok_dev * width * (width + 3 * size),
            8 * tok_dev * width + 2 * width * width + 6 * size * width,
            tok_dev * width,
        ),
        name="apply_fast",
    )(position, *gathered, *units, *attends, norm_gain, output_weight)


def body(
    activations,
    view_id,
    window_lengths,
    project_weight,
    rate_weight,
    fast_start,
    momentum,
    norm_gain,
    output_weight,
):
    tok_dev, width = activations.shape
    shards = lax.axis_size("tok")
    index = lax.axis_index("tok")
    position = index.reshape(1).astype(jnp.int32)
    heads = rate_weight.shape[1]
    size = width // heads
    slab = size // shards

    def swap(array, bit):
        return lax.ppermute(array, "tok", [(i, i ^ bit) for i in range(shards)])

    sent = group_by_view(view_id, activations, shards)
    arrived = lax.all_to_all(
        sent.reshape(shards, tok_dev // shards, width), "tok", split_axis=0, concat_axis=0, tiled=True
    ).reshape(tok_dev, width)
    ends = jnp.cumsum(window_lengths[0])
    own_start = lax.dynamic_slice_in_dim(fast_start, index * slab, slab, 0)

    keep, send = fast_gradient(
        position, after(activations, sent), project_weight, rate_weight, fast_start, shards
    )
    units, attends = [], []
    bit = 1
    while bit < shards:
        received = swap(send, bit)
        if bit == 8:
            unit, attended = project_and_attend(ends, after(arrived, send), project_weight, heads, 0, 1)
            units.append(unit)
            attends.append(attended)
            done = 1
            received = after(received, attended)
        bit *= 2
        if bit < shards:
            keep, send = add_and_halve(keep, received)
    momentum_next, block = update_rows(keep, received, momentum, own_start)

    stages = shards.bit_length() - 1
    bit = shards // 2
    for stage in range(stages - 1):
        last = stage == stages - 2
        count = heads - done if last else min(1, heads - done)
        if count:
            unit, attended = project_and_attend(
                ends, after(arrived, block), project_weight, heads, done, count
            )
            units.append(unit)
            attends.append(attended)
            done += count
        other = swap(block, bit)
        if not last:
            block = join(block, after(other, attends[-1]))
            bit //= 2
    gathered = [block, other, swap(block, 1), swap(after(other, attends[-1]), 1)]
    mixed = apply_fast(position, gathered, units, attends, norm_gain, output_weight, shards)
    return (mixed[None], momentum_next)


def solution(mesh):
    in_specs = (
        P(("group", "tok"), None),
        P(("group", "tok")),
        P(("group", "tok"), None),
        P(),
        P(),
        P(),
        P(("group", "tok"), None, None, None),
        P(),
        P(),
    )
    out_specs = (P(("group", "tok"), None, None), P(("group", "tok"), None, None, None))
    return jax.shard_map(body, mesh=mesh, in_specs=in_specs, out_specs=out_specs, check_vma=False)
```

```python
import math

import jax
import jax.numpy as jnp
from jax import lax
from jax.experimental import pallas as pl
from jax.experimental.pallas import tpu as pltpu
from jax.sharding import PartitionSpec as P

F32 = jnp.float32
BF16 = jnp.bfloat16
MIB = 1024 * 1024


def dot(a, b):
    return jnp.dot(a, b, preferred_element_type=F32)


def dot_tn(a, b):
    return lax.dot_general(a, b, (((0,), (0,)), ((), ())), preferred_element_type=F32)


def dot_nt(a, b):
    return lax.dot_general(a, b, (((1,), (1,)), ((), ())), preferred_element_type=F32)


def bit_reverse(value, width):
    out = 0
    for bit in range(width):
        out |= ((value >> bit) & 1) << (width - 1 - bit)
    return out


def params(mebibytes):
    return pltpu.CompilerParams(
        dimension_semantics=("arbitrary",), vmem_limit_bytes=mebibytes * MIB
    )


def after(array, *others):
    return lax.optimization_barrier((array, *others))[0]


def cost(flops, nbytes, transcendentals=0):
    return pl.CostEstimate(
        flops=int(flops), bytes_accessed=int(nbytes), transcendentals=int(transcendentals)
    )


def group_by_view(view_id, activations, shards):
    tok_dev, width = activations.shape
    per_view = tok_dev // shards
    chunk = 256
    tile = 1024

    def kernel(view_ref, act_ref, out_ref, slot_ref):
        @pl.when(pl.program_id(0) == 0)
        def _():
            rows = lax.broadcasted_iota(jnp.int32, (chunk, chunk), 0)
            cols = lax.broadcasted_iota(jnp.int32, (chunk, chunk), 1)
            upper = jnp.where(rows < cols, 1.0, 0.0).astype(BF16)
            views = lax.broadcasted_iota(jnp.int32, (shards, chunk), 0)
            before = jnp.zeros((shards, 1), F32)
            for start in range(0, tok_dev, chunk):
                member = views == view_ref[:, start : start + chunk]
                hot = jnp.where(member, 1.0, 0.0)
                rank = dot(hot.astype(BF16), upper) + before
                slot = jnp.where(member, rank + (views * per_view).astype(F32), 0.0)
                slot_ref[:, start : start + chunk] = jnp.sum(slot, axis=0, keepdims=True).astype(
                    jnp.int32
                )
                before = before + jnp.sum(hot, axis=1, keepdims=True)

        target = lax.broadcasted_iota(jnp.int32, (tile, tok_dev), 0) + pl.program_id(0) * tile
        pick = jnp.where(target == slot_ref[...], 1.0, 0.0).astype(BF16)
        out_ref[...] = dot(pick, act_ref[...]).astype(BF16)

    return pl.pallas_call(
        kernel,
        grid=(tok_dev // tile,),
        in_specs=[
            pl.BlockSpec((1, tok_dev), lambda i: (0, 0)),
            pl.BlockSpec((tok_dev, width), lambda i: (0, 0)),
        ],
        out_specs=pl.BlockSpec((tile, width), lambda i: (i, 0)),
        out_shape=jax.ShapeDtypeStruct((tok_dev, width), BF16),
        scratch_shapes=[pltpu.VMEM((1, tok_dev), jnp.int32)],
        compiler_params=params(60),
        cost_estimate=cost(2 * tok_dev * tok_dev * width, 4 * tok_dev * width),
        name="group_by_view",
    )(view_id.reshape(1, tok_dev), activations)


def fast_gradient(position, activations, project_weight, rate_weight, fast_start, shards):
    tok_dev, width = activations.shape
    heads = rate_weight.shape[1]
    kinds = fast_start.shape[1]
    size = width // heads
    slab = size // shards
    stages = shards.bit_length() - 1
    tile = 1024
    scale = 0.1 / math.sqrt(tok_dev * shards)
    half = size // 2

    def kernel(pos_ref, act_ref, wk_ref, wv_ref, rate_w_ref, fast_ref, keep_ref, send_ref,
               rate_ref, key_ref, out_ref, hid_ref, gate_ref, grad_ref, start_ref, sems):
        head = pl.program_id(0)
        slot = head % 2

        def fetch(which, place):
            return [
                pltpu.make_async_copy(
                    fast_ref.at[:, kind, which, :], start_ref.at[place, kind], sems.at[place, kind]
                )
                for kind in range(kinds)
            ]

        @pl.when(head == 0)
        def _():
            for copy in fetch(0, 0):
                copy.start()
            raw = dot_nt(act_ref[...], rate_w_ref[...])
            rate_ref[...] = (jnp.maximum(raw, 0.0) + jnp.log1p(jnp.exp(-jnp.abs(raw)))) * scale

        @pl.when(head + 1 < heads)
        def _():
            for copy in fetch(head + 1, 1 - slot):
                copy.start()

        for copy in fetch(head, slot):
            copy.wait()
        w_gate, w_up, w_down = [start_ref[slot, kind].astype(BF16) for kind in range(kinds)]
        for start in range(0, tok_dev, tile):
            rows = slice(start, start + tile)
            act = act_ref[rows, :]
            keys = dot(act, wk_ref[...]).astype(BF16).astype(F32)
            values = dot(act, wv_ref[...]).astype(BF16).astype(F32)
            key_unit = (
                keys * lax.rsqrt(jnp.mean(keys * keys, axis=-1, keepdims=True) + 1e-06)
            ).astype(BF16)
            lanes = lax.broadcasted_iota(jnp.int32, (tile, heads), 1)
            rate = jnp.sum(
                jnp.where(lanes == head, rate_ref[rows, :], 0.0), axis=1, keepdims=True
            )
            back_out = (-rate * values).astype(BF16)
            pre_gate = dot(key_unit, w_gate)
            pre_up = dot(key_unit, w_up)
            back_hidden = dot(back_out, w_down)
            sig = jax.nn.sigmoid(pre_gate)
            act_gate = pre_gate * sig
            key_ref[rows, :] = key_unit
            out_ref[rows, :] = back_out
            hid_ref[rows, :] = (act_gate * pre_up).astype(BF16)
            gate_ref[rows, 0:size] = (
                back_hidden * pre_up * sig * (1.0 + pre_gate * (1.0 - sig))
            ).astype(BF16)
            gate_ref[rows, size : 2 * size] = (back_hidden * act_gate).astype(BF16)
        grad_ref[:, 0 : 2 * size] = dot_tn(key_ref[...], gate_ref[...])
        grad_ref[:, 2 * size : 3 * size] = dot_tn(out_ref[...], hid_ref[...])
        for place in range(shards):
            owner = pos_ref[0] ^ bit_reverse(place, stages)
            rows = grad_ref[pl.ds(pl.multiple_of(owner * slab, slab), slab), :]
            if place < shards // 2:
                keep_ref[place * slab : (place + 1) * slab, :] = rows
            else:
                low = place * slab - half
                send_ref[low : low + slab, :] = rows.astype(BF16)

    return pl.pallas_call(
        kernel,
        grid_spec=pltpu.PrefetchScalarGridSpec(
            num_scalar_prefetch=1,
            grid=(heads,),
            in_specs=[
                pl.BlockSpec((tok_dev, width), lambda h, p: (0, 0)),
                pl.BlockSpec((width, size), lambda h, p: (0, heads + h)),
                pl.BlockSpec((width, size), lambda h, p: (0, 2 * heads + h)),
                pl.BlockSpec((heads, width), lambda h, p: (0, 0)),
                pl.BlockSpec(memory_space=pl.ANY),
            ],
            out_specs=[
                pl.BlockSpec((half, 3 * size), lambda h, p: (0, h)),
                pl.BlockSpec((half, 3 * size), lambda h, p: (0, h)),
            ],
            scratch_shapes=[
                pltpu.VMEM((tok_dev, heads), F32),
                pltpu.VMEM((tok_dev, size), BF16),
                pltpu.VMEM((tok_dev, size), BF16),
                pltpu.VMEM((tok_dev, size), BF16),
                pltpu.VMEM((tok_dev, 2 * size), BF16),
                pltpu.VMEM((size, 3 * size), F32),
                pltpu.VMEM((2, kinds, size, size), F32),
                pltpu.SemaphoreType.DMA((2, kinds)),
            ],
        ),
        out_shape=[
            jax.ShapeDtypeStruct((half, 3 * width), F32),
            jax.ShapeDtypeStruct((half, 3 * width), BF16),
        ],
        compiler_params=params(60),
        cost_estimate=cost(
            2 * tok_dev * width * (2 * width + 6 * size),
            2 * tok_dev * width + 4 * width * width + 6 * size * width + 9 * size * width,
            4 * tok_dev * width,
        ),
        name="fast_gradient",
    )(position, activations, project_weight, project_weight, rate_weight.T, fast_start)


def add_and_halve(keep, received):
    rows, width = keep.shape
    half = rows // 2

    def kernel(keep_ref, got_ref, stay_ref, go_ref):
        stay_ref[...] = keep_ref[:half, :] + got_ref[:half, :].astype(F32)
        go_ref[...] = (keep_ref[half:, :] + got_ref[half:, :].astype(F32)).astype(BF16)

    whole = pl.BlockSpec(memory_space=pltpu.VMEM)
    return pl.pallas_call(
        kernel,
        in_specs=[whole, whole],
        out_specs=[whole, whole],
        out_shape=[
            jax.ShapeDtypeStruct((half, width), F32),
            jax.ShapeDtypeStruct((half, width), BF16),
        ],
        compiler_params=pltpu.CompilerParams(vmem_limit_bytes=6 * MIB),
        cost_estimate=cost(rows * width, 9 * rows * width),
        name="add_and_halve",
    )(keep, received)


def join(first, second):
    rows, width = first.shape

    def kernel(first_ref, second_ref, out_ref):
        out_ref[:rows, :] = first_ref[...]
        out_ref[rows:, :] = second_ref[...]

    whole = pl.BlockSpec(memory_space=pltpu.VMEM)
    return pl.pallas_call(
        kernel,
        in_specs=[whole, whole],
        out_specs=whole,
        out_shape=jax.ShapeDtypeStruct((2 * rows, width), BF16),
        compiler_params=pltpu.CompilerParams(vmem_limit_bytes=4 * MIB),
        cost_estimate=cost(0, 8 * rows * width),
        name="join",
    )(first, second)


def update_rows(keep, received, momentum, own_start):
    rows, kinds, heads, size = momentum.shape
    width = keep.shape[1]

    def kernel(keep_ref, got_ref, mom_ref, start_ref, next_ref, share_ref):
        for head in range(heads):
            for kind in range(kinds):
                low = (head * kinds + kind) * size
                cols = slice(low, low + size)
                moment = 0.9 * mom_ref[:, kind, head, :] + (
                    keep_ref[:, cols] + got_ref[:, cols].astype(F32)
                )
                next_ref[:, kind, head, :] = moment
                start = start_ref[:, kind, head, :]
                moved = start - moment
                factor = jnp.sqrt(jnp.sum(start * start, axis=-1, keepdims=True)) / jnp.sqrt(
                    jnp.sum(moved * moved, axis=-1, keepdims=True) + 1e-06
                )
                share_ref[:, cols] = (moved * factor).astype(BF16)

    whole = pl.BlockSpec(memory_space=pltpu.VMEM)
    return pl.pallas_call(
        kernel,
        in_specs=[whole] * 4,
        out_specs=[whole, whole],
        out_shape=[
            jax.ShapeDtypeStruct(momentum.shape, F32),
            jax.ShapeDtypeStruct((rows, width), BF16),
        ],
        compiler_params=pltpu.CompilerParams(vmem_limit_bytes=4 * MIB),
        cost_estimate=cost(8 * rows * width, 20 * rows * width),
        name="update_rows",
    )(keep, received, momentum, own_start)


def head_weights(project_weight, heads, head):
    width, columns = project_weight.shape
    kinds = 3
    size = columns // kinds // heads

    def kernel(in_ref, out_ref):
        out_ref[...] = in_ref[...]

    return pl.pallas_call(
        kernel,
        grid=(kinds,),
        in_specs=[pl.BlockSpec((width, size), lambda kind: (0, kind * heads + head))],
        out_specs=pl.BlockSpec((width, size), lambda kind: (0, kind)),
        out_shape=jax.ShapeDtypeStruct((width, kinds * size), BF16),
        compiler_params=params(8),
        cost_estimate=cost(0, 4 * width * kinds * size),
        name="head_weights",
    )(project_weight)


def project_and_attend(window_ends, arrived, weights):
    tok_dev, width = arrived.shape
    size = weights.shape[1] // 3
    count = 1
    windows = window_ends.shape[0]
    tile = 512
    scale = math.log2(math.e) / math.sqrt(size)

    def kernel(ends_ref, x_ref, weight_ref, unit_ref, att_ref):
        x = x_ref[...]
        queries = dot(x, weight_ref[:, 0:size]).astype(BF16)
        keys = dot(x, weight_ref[:, size : 2 * size]).astype(BF16)
        values = dot(x, weight_ref[:, 2 * size : 3 * size]).astype(BF16)
        wide = queries.astype(F32)
        unit_ref[...] = (
            wide * lax.rsqrt(jnp.mean(wide * wide, axis=-1, keepdims=True) + 1e-06)
        ).astype(BF16)
        key_place = lax.broadcasted_iota(jnp.int32, (1, tok_dev), 1)
        key_window = jnp.zeros((1, tok_dev), jnp.int32)
        for w in range(windows):
            key_window += (key_place >= ends_ref[w]).astype(jnp.int32)
        for start in range(0, tok_dev, tile):
            place = lax.broadcasted_iota(jnp.int32, (tile, 1), 0) + start
            window = jnp.zeros((tile, 1), jnp.int32)
            for w in range(windows):
                window += (place >= ends_ref[w]).astype(jnp.int32)
            scores = dot_nt(queries[start : start + tile], keys)
            scores = jnp.where(window == key_window, scores, -1e30)
            highest = jnp.max(scores, axis=-1, keepdims=True)
            expo = jnp.exp2((scores - highest) * scale)
            total = jnp.sum(expo, axis=-1, keepdims=True)
            att_ref[start : start + tile, :] = dot(expo.astype(BF16), values) * (
                1.0 / total
            )

    return pl.pallas_call(
        kernel,
        grid_spec=pltpu.PrefetchScalarGridSpec(
            num_scalar_prefetch=1,
            grid=(count,),
            in_specs=[
                pl.BlockSpec((tok_dev, width), lambda h, e: (0, 0)),
                pl.BlockSpec((width, 3 * size), lambda h, e: (0, 0)),
            ],
            out_specs=[
                pl.BlockSpec((tok_dev, size), lambda h, e: (0, h)),
                pl.BlockSpec((tok_dev, size), lambda h, e: (0, h)),
            ],
        ),
        out_shape=[
            jax.ShapeDtypeStruct((tok_dev, count * size), BF16),
            jax.ShapeDtypeStruct((tok_dev, count * size), F32),
        ],
        compiler_params=params(34),
        cost_estimate=cost(
            2 * tok_dev * count * size * (3 * width + 2 * tok_dev),
            2 * tok_dev * width + 6 * tok_dev * count * size + 6 * width * count * size,
            count * tok_dev * tok_dev,
        ),
        name="project_and_attend",
    )(window_ends, arrived, weights)


def apply_fast(position, gathered, units, attends, norm_gain, output_weight, shards):
    tok_dev = units[0].shape[0]
    width = output_weight.shape[0]
    heads, size = norm_gain.shape
    slab = size // shards
    stages = shards.bit_length() - 1
    tile = 1024
    parts = len(gathered)
    part_rows = size // parts
    pieces_of = len(units)
    where = []
    for piece, unit in enumerate(units):
        where += [(piece, low) for low in range(0, unit.shape[1], size)]

    def kernel(pos_ref, *refs):
        part_refs = refs[:parts]
        unit_refs = refs[parts : parts + pieces_of]
        att_refs = refs[parts + pieces_of : parts + 2 * pieces_of]
        gain_ref, ow_ref, mix_ref, wide_ref, fast_ref = refs[parts + 2 * pieces_of :]

        @pl.when(pl.program_id(0) == 0)
        def _():
            for place in range(shards):
                owner = pos_ref[0] ^ bit_reverse(place, stages)
                low = (place * slab) % part_rows
                rows = part_refs[place * slab // part_rows][low : low + slab, :]
                wide_ref[pl.ds(pl.multiple_of(owner * slab, slab), slab), :] = rows.astype(F32)
            fast_ref[...] = wide_ref[...].astype(BF16)

        pieces = []
        for head in range(heads):
            low = head * 3 * size
            piece, col = where[head]
            cols = slice(col, col + size)
            query = unit_refs[piece][:, cols]
            gate = dot(query, fast_ref[:, low : low + size])
            up = dot(query, fast_ref[:, low + size : low + 2 * size])
            hidden = (gate * jax.nn.sigmoid(gate) * up).astype(BF16)
            out = dot_nt(hidden, fast_ref[:, low + 2 * size : low + 3 * size])
            out = out * lax.rsqrt(jnp.mean(out * out, axis=-1, keepdims=True) + 1e-06)
            normed = (out * gain_ref[head : head + 1, :]).astype(BF16).astype(F32)
            pieces.append((normed + att_refs[piece][:, cols]).astype(BF16))
        combined = jnp.concatenate(pieces, axis=1)
        mix_ref[...] = dot(combined, ow_ref[...]).astype(BF16)

    return pl.pallas_call(
        kernel,
        grid_spec=pltpu.PrefetchScalarGridSpec(
            num_scalar_prefetch=1,
            grid=(tok_dev // tile,),
            in_specs=[pl.BlockSpec((part_rows, 3 * width), lambda i, p: (0, 0))] * parts
            + [pl.BlockSpec((tile, unit.shape[1]), lambda i, p: (i, 0)) for unit in units] * 2
            + [
                pl.BlockSpec((heads, size), lambda i, p: (0, 0)),
                pl.BlockSpec((width, width), lambda i, p: (0, 0)),
            ],
            out_specs=pl.BlockSpec((tile, width), lambda i, p: (i, 0)),
            scratch_shapes=[
                pltpu.VMEM((size, 3 * width), F32),
                pltpu.VMEM((size, 3 * width), BF16),
            ],
        ),
        out_shape=jax.ShapeDtypeStruct((tok_dev, width), BF16),
        compiler_params=params(40),
        cost_estimate=cost(
            2 * tok_dev * width * (width + 3 * size),
            8 * tok_dev * width + 2 * width * width + 6 * size * width,
            tok_dev * width,
        ),
        name="apply_fast",
    )(position, *gathered, *units, *attends, norm_gain, output_weight)


def body(
    activations,
    view_id,
    window_lengths,
    project_weight,
    rate_weight,
    fast_start,
    momentum,
    norm_gain,
    output_weight,
):
    tok_dev, width = activations.shape
    shards = lax.axis_size("tok")
    index = lax.axis_index("tok")
    position = index.reshape(1).astype(jnp.int32)
    heads = rate_weight.shape[1]
    size = width // heads
    slab = size // shards

    def swap(array, bit):
        return lax.ppermute(array, "tok", [(i, i ^ bit) for i in range(shards)])

    sent = group_by_view(view_id, activations, shards)
    arrived = lax.all_to_all(
        sent.reshape(shards, tok_dev // shards, width), "tok", split_axis=0, concat_axis=0, tiled=True
    ).reshape(tok_dev, width)
    ends = jnp.cumsum(window_lengths[0])
    own_start = lax.dynamic_slice_in_dim(fast_start, index * slab, slab, 0)

    keep, send = fast_gradient(
        position, after(activations, sent), project_weight, rate_weight, fast_start, shards
    )
    units, attends = [], []
    bit = 1
    while bit < shards:
        received = swap(send, bit)
        if bit == 2:
            source = after(project_weight, send)
            held = [head_weights(source, heads, head) for head in range(heads)]
            received = after(received, *held)
        if bit == 8:
            unit, attended = project_and_attend(ends, after(arrived, send), held[0])
            units.append(unit)
            attends.append(attended)
            received = after(received, attended)
        bit *= 2
        if bit < shards:
            keep, send = add_and_halve(keep, received)
    momentum_next, block = update_rows(keep, received, momentum, own_start)

    def attend(count, *others):
        first = len(units)
        for head in range(first, min(first + count, heads)):
            unit, attended = project_and_attend(ends, after(arrived, *others), held[head])
            units.append(unit)
            attends.append(attended)

    bit = shards // 2
    while bit > 4:
        attend(1, block)
        block = join(block, after(swap(block, bit), attends[-1]))
        bit //= 2
    attend(1, block)
    own = {0: block, 4: swap(block, 4), 2: swap(block, 2)}
    other = {0: swap(block, 1)}
    last = after(own[4], attends[-1])
    own[6] = swap(last, 2)
    other[4] = swap(last, 1)
    other[2] = swap(after(own[2], attends[-1]), 1)
    attend(heads, last)
    other[6] = swap(after(own[6], attends[-1]), 1)
    gathered = [side[place] for side in (own, other) for place in (0, 4, 2, 6)]
    mixed = apply_fast(position, gathered, units, attends, norm_gain, output_weight, shards)
    return (mixed[None], momentum_next)


def solution(mesh):
    in_specs = (
        P(("group", "tok"), None),
        P(("group", "tok")),
        P(("group", "tok"), None),
        P(),
        P(),
        P(),
        P(("group", "tok"), None, None, None),
        P(),
        P(),
    )
    out_specs = (P(("group", "tok"), None, None), P(("group", "tok"), None, None, None))
    return jax.shard_map(body, mesh=mesh, in_specs=in_specs, out_specs=out_specs, check_vma=False)
```

```python
import math

import jax
import jax.numpy as jnp
from jax import lax
from jax.experimental import pallas as pl
from jax.experimental.pallas import tpu as pltpu
from jax.sharding import PartitionSpec as P

F32 = jnp.float32
BF16 = jnp.bfloat16
MIB = 1024 * 1024


def dot(a, b):
    return jnp.dot(a, b, preferred_element_type=F32)


def dot_tn(a, b):
    return lax.dot_general(a, b, (((0,), (0,)), ((), ())), preferred_element_type=F32)


def dot_nt(a, b):
    return lax.dot_general(a, b, (((1,), (1,)), ((), ())), preferred_element_type=F32)


def bit_reverse(value, width):
    out = 0
    for bit in range(width):
        out |= ((value >> bit) & 1) << (width - 1 - bit)
    return out


def params(mebibytes):
    return pltpu.CompilerParams(
        dimension_semantics=("arbitrary",), vmem_limit_bytes=mebibytes * MIB
    )


def after(array, *others):
    return lax.optimization_barrier((array, *others))[0]


def cost(flops, nbytes, transcendentals=0):
    return pl.CostEstimate(
        flops=int(flops), bytes_accessed=int(nbytes), transcendentals=int(transcendentals)
    )


def group_by_view(view_id, activations, shards):
    tok_dev, width = activations.shape
    per_view = tok_dev // shards
    chunk = 256
    tile = 1024

    def kernel(view_ref, act_ref, out_ref, slot_ref):
        @pl.when(pl.program_id(0) == 0)
        def _():
            rows = lax.broadcasted_iota(jnp.int32, (chunk, chunk), 0)
            cols = lax.broadcasted_iota(jnp.int32, (chunk, chunk), 1)
            upper = jnp.where(rows < cols, 1.0, 0.0).astype(BF16)
            views = lax.broadcasted_iota(jnp.int32, (shards, chunk), 0)
            before = jnp.zeros((shards, 1), F32)
            for start in range(0, tok_dev, chunk):
                member = views == view_ref[:, start : start + chunk]
                hot = jnp.where(member, 1.0, 0.0)
                rank = dot(hot.astype(BF16), upper) + before
                slot = jnp.where(member, rank + (views * per_view).astype(F32), 0.0)
                slot_ref[:, start : start + chunk] = jnp.sum(slot, axis=0, keepdims=True).astype(
                    jnp.int32
                )
                before = before + jnp.sum(hot, axis=1, keepdims=True)

        target = lax.broadcasted_iota(jnp.int32, (tile, tok_dev), 0) + pl.program_id(0) * tile
        pick = jnp.where(target == slot_ref[...], 1.0, 0.0).astype(BF16)
        out_ref[...] = dot(pick, act_ref[...]).astype(BF16)

    return pl.pallas_call(
        kernel,
        grid=(tok_dev // tile,),
        in_specs=[
            pl.BlockSpec((1, tok_dev), lambda i: (0, 0)),
            pl.BlockSpec((tok_dev, width), lambda i: (0, 0)),
        ],
        out_specs=pl.BlockSpec((tile, width), lambda i: (i, 0)),
        out_shape=jax.ShapeDtypeStruct((tok_dev, width), BF16),
        scratch_shapes=[pltpu.VMEM((1, tok_dev), jnp.int32)],
        compiler_params=params(60),
        cost_estimate=cost(2 * tok_dev * tok_dev * width, 4 * tok_dev * width),
        name="group_by_view",
    )(view_id.reshape(1, tok_dev), activations)


def fast_gradient(position, activations, project_weight, rate_weight, fast_start, shards):
    tok_dev, width = activations.shape
    heads = rate_weight.shape[1]
    kinds = fast_start.shape[1]
    size = width // heads
    slab = size // shards
    stages = shards.bit_length() - 1
    tile = 1024
    scale = 0.1 / math.sqrt(tok_dev * shards)
    half = size // 2

    def kernel(pos_ref, act_ref, wk_ref, wv_ref, rate_w_ref, fast_ref, keep_ref, send_ref,
               rate_ref, key_ref, out_ref, hid_ref, gate_ref, grad_ref, start_ref, sems):
        head = pl.program_id(0)
        slot = head % 2

        def fetch(which, place):
            return [
                pltpu.make_async_copy(
                    fast_ref.at[:, kind, which, :], start_ref.at[place, kind], sems.at[place, kind]
                )
                for kind in range(kinds)
            ]

        @pl.when(head == 0)
        def _():
            for copy in fetch(0, 0):
                copy.start()
            raw = dot_nt(act_ref[...], rate_w_ref[...])
            rate_ref[...] = (jnp.maximum(raw, 0.0) + jnp.log1p(jnp.exp(-jnp.abs(raw)))) * scale

        @pl.when(head + 1 < heads)
        def _():
            for copy in fetch(head + 1, 1 - slot):
                copy.start()

        for copy in fetch(head, slot):
            copy.wait()
        w_gate, w_up, w_down = [start_ref[slot, kind].astype(BF16) for kind in range(kinds)]
        for start in range(0, tok_dev, tile):
            rows = slice(start, start + tile)
            act = act_ref[rows, :]
            keys = dot(act, wk_ref[...]).astype(BF16).astype(F32)
            values = dot(act, wv_ref[...]).astype(BF16).astype(F32)
            key_unit = (
                keys * lax.rsqrt(jnp.mean(keys * keys, axis=-1, keepdims=True) + 1e-06)
            ).astype(BF16)
            lanes = lax.broadcasted_iota(jnp.int32, (tile, heads), 1)
            rate = jnp.sum(
                jnp.where(lanes == head, rate_ref[rows, :], 0.0), axis=1, keepdims=True
            )
            back_out = (-rate * values).astype(BF16)
            pre_gate = dot(key_unit, w_gate)
            pre_up = dot(key_unit, w_up)
            back_hidden = dot(back_out, w_down)
            sig = jax.nn.sigmoid(pre_gate)
            act_gate = pre_gate * sig
            key_ref[rows, :] = key_unit
            out_ref[rows, :] = back_out
            hid_ref[rows, :] = (act_gate * pre_up).astype(BF16)
            gate_ref[rows, 0:size] = (
                back_hidden * pre_up * sig * (1.0 + pre_gate * (1.0 - sig))
            ).astype(BF16)
            gate_ref[rows, size : 2 * size] = (back_hidden * act_gate).astype(BF16)
        grad_ref[:, 0 : 2 * size] = dot_tn(key_ref[...], gate_ref[...])
        grad_ref[:, 2 * size : 3 * size] = dot_tn(out_ref[...], hid_ref[...])
        for place in range(shards):
            owner = pos_ref[0] ^ bit_reverse(place, stages)
            rows = grad_ref[pl.ds(pl.multiple_of(owner * slab, slab), slab), :]
            if place < shards // 2:
                keep_ref[place * slab : (place + 1) * slab, :] = rows
            else:
                low = place * slab - half
                send_ref[low : low + slab, :] = rows.astype(BF16)

    return pl.pallas_call(
        kernel,
        grid_spec=pltpu.PrefetchScalarGridSpec(
            num_scalar_prefetch=1,
            grid=(heads,),
            in_specs=[
                pl.BlockSpec((tok_dev, width), lambda h, p: (0, 0)),
                pl.BlockSpec((width, size), lambda h, p: (0, heads + h)),
                pl.BlockSpec((width, size), lambda h, p: (0, 2 * heads + h)),
                pl.BlockSpec((heads, width), lambda h, p: (0, 0)),
                pl.BlockSpec(memory_space=pl.ANY),
            ],
            out_specs=[
                pl.BlockSpec((half, 3 * size), lambda h, p: (0, h)),
                pl.BlockSpec((half, 3 * size), lambda h, p: (0, h)),
            ],
            scratch_shapes=[
                pltpu.VMEM((tok_dev, heads), F32),
                pltpu.VMEM((tok_dev, size), BF16),
                pltpu.VMEM((tok_dev, size), BF16),
                pltpu.VMEM((tok_dev, size), BF16),
                pltpu.VMEM((tok_dev, 2 * size), BF16),
                pltpu.VMEM((size, 3 * size), F32),
                pltpu.VMEM((2, kinds, size, size), F32),
                pltpu.SemaphoreType.DMA((2, kinds)),
            ],
        ),
        out_shape=[
            jax.ShapeDtypeStruct((half, 3 * width), F32),
            jax.ShapeDtypeStruct((half, 3 * width), BF16),
        ],
        compiler_params=params(60),
        cost_estimate=cost(
            2 * tok_dev * width * (2 * width + 6 * size),
            2 * tok_dev * width + 4 * width * width + 6 * size * width + 9 * size * width,
            4 * tok_dev * width,
        ),
        name="fast_gradient",
    )(position, activations, project_weight, project_weight, rate_weight.T, fast_start)


def add_and_halve(keep, received):
    rows, width = keep.shape
    half = rows // 2

    def kernel(keep_ref, got_ref, stay_ref, go_ref):
        stay_ref[...] = keep_ref[:half, :] + got_ref[:half, :].astype(F32)
        go_ref[...] = (keep_ref[half:, :] + got_ref[half:, :].astype(F32)).astype(BF16)

    whole = pl.BlockSpec(memory_space=pltpu.VMEM)
    return pl.pallas_call(
        kernel,
        in_specs=[whole, whole],
        out_specs=[whole, whole],
        out_shape=[
            jax.ShapeDtypeStruct((half, width), F32),
            jax.ShapeDtypeStruct((half, width), BF16),
        ],
        compiler_params=pltpu.CompilerParams(vmem_limit_bytes=6 * MIB),
        cost_estimate=cost(rows * width, 9 * rows * width),
        name="add_and_halve",
    )(keep, received)


def join(first, second):
    rows, width = first.shape

    def kernel(first_ref, second_ref, out_ref):
        out_ref[:rows, :] = first_ref[...]
        out_ref[rows:, :] = second_ref[...]

    whole = pl.BlockSpec(memory_space=pltpu.VMEM)
    return pl.pallas_call(
        kernel,
        in_specs=[whole, whole],
        out_specs=whole,
        out_shape=jax.ShapeDtypeStruct((2 * rows, width), BF16),
        compiler_params=pltpu.CompilerParams(vmem_limit_bytes=4 * MIB),
        cost_estimate=cost(0, 8 * rows * width),
        name="join",
    )(first, second)


def update_rows(keep, received, momentum, own_start):
    rows, kinds, heads, size = momentum.shape
    width = keep.shape[1]

    def kernel(keep_ref, got_ref, mom_ref, start_ref, next_ref, share_ref):
        for head in range(heads):
            for kind in range(kinds):
                low = (head * kinds + kind) * size
                cols = slice(low, low + size)
                moment = 0.9 * mom_ref[:, kind, head, :] + (
                    keep_ref[:, cols] + got_ref[:, cols].astype(F32)
                )
                next_ref[:, kind, head, :] = moment
                start = start_ref[:, kind, head, :]
                moved = start - moment
                factor = jnp.sqrt(jnp.sum(start * start, axis=-1, keepdims=True)) / jnp.sqrt(
                    jnp.sum(moved * moved, axis=-1, keepdims=True) + 1e-06
                )
                share_ref[:, cols] = (moved * factor).astype(BF16)

    whole = pl.BlockSpec(memory_space=pltpu.VMEM)
    return pl.pallas_call(
        kernel,
        in_specs=[whole] * 4,
        out_specs=[whole, whole],
        out_shape=[
            jax.ShapeDtypeStruct(momentum.shape, F32),
            jax.ShapeDtypeStruct((rows, width), BF16),
        ],
        compiler_params=pltpu.CompilerParams(vmem_limit_bytes=4 * MIB),
        cost_estimate=cost(8 * rows * width, 20 * rows * width),
        name="update_rows",
    )(keep, received, momentum, own_start)


def head_weights(project_weight, heads, head):
    width, columns = project_weight.shape
    kinds = 3
    size = columns // kinds // heads

    def kernel(in_ref, out_ref):
        out_ref[...] = in_ref[...]

    return pl.pallas_call(
        kernel,
        grid=(kinds,),
        in_specs=[pl.BlockSpec((width, size), lambda kind: (0, kind * heads + head))],
        out_specs=pl.BlockSpec((width, size), lambda kind: (0, kind)),
        out_shape=jax.ShapeDtypeStruct((width, kinds * size), BF16),
        compiler_params=params(8),
        cost_estimate=cost(0, 4 * width * kinds * size),
        name="head_weights",
    )(project_weight)


def project_and_attend(window_ends, arrived, weights):
    tok_dev, width = arrived.shape
    size = weights.shape[1] // 3
    count = 1
    windows = window_ends.shape[0]
    tile = 512
    scale = math.log2(math.e) / math.sqrt(size)

    def kernel(ends_ref, x_ref, weight_ref, unit_ref, att_ref):
        x = x_ref[...]
        queries = dot(x, weight_ref[:, 0:size]).astype(BF16)
        keys = dot(x, weight_ref[:, size : 2 * size]).astype(BF16)
        values = dot(x, weight_ref[:, 2 * size : 3 * size]).astype(BF16)
        wide = queries.astype(F32)
        unit_ref[...] = (
            wide * lax.rsqrt(jnp.mean(wide * wide, axis=-1, keepdims=True) + 1e-06)
        ).astype(BF16)
        key_place = lax.broadcasted_iota(jnp.int32, (1, tok_dev), 1)
        key_window = jnp.zeros((1, tok_dev), jnp.int32)
        for w in range(windows):
            key_window += (key_place >= ends_ref[w]).astype(jnp.int32)
        for start in range(0, tok_dev, tile):
            place = lax.broadcasted_iota(jnp.int32, (tile, 1), 0) + start
            window = jnp.zeros((tile, 1), jnp.int32)
            for w in range(windows):
                window += (place >= ends_ref[w]).astype(jnp.int32)
            scores = dot_nt(queries[start : start + tile], keys)
            scores = jnp.where(window == key_window, scores, -1e30)
            highest = jnp.max(scores, axis=-1, keepdims=True)
            expo = jnp.exp2((scores - highest) * scale)
            total = jnp.sum(expo, axis=-1, keepdims=True)
            att_ref[start : start + tile, :] = dot(expo.astype(BF16), values) * (
                1.0 / total
            )

    return pl.pallas_call(
        kernel,
        grid_spec=pltpu.PrefetchScalarGridSpec(
            num_scalar_prefetch=1,
            grid=(count,),
            in_specs=[
                pl.BlockSpec((tok_dev, width), lambda h, e: (0, 0)),
                pl.BlockSpec((width, 3 * size), lambda h, e: (0, 0)),
            ],
            out_specs=[
                pl.BlockSpec((tok_dev, size), lambda h, e: (0, h)),
                pl.BlockSpec((tok_dev, size), lambda h, e: (0, h)),
            ],
        ),
        out_shape=[
            jax.ShapeDtypeStruct((tok_dev, count * size), BF16),
            jax.ShapeDtypeStruct((tok_dev, count * size), F32),
        ],
        compiler_params=params(34),
        cost_estimate=cost(
            2 * tok_dev * count * size * (3 * width + 2 * tok_dev),
            2 * tok_dev * width + 6 * tok_dev * count * size + 6 * width * count * size,
            count * tok_dev * tok_dev,
        ),
        name="project_and_attend",
    )(window_ends, arrived, weights)


def apply_fast(position, gathered, units, attends, norm_gain, output_weight, shards):
    tok_dev = units[0].shape[0]
    width = output_weight.shape[0]
    heads, size = norm_gain.shape
    slab = size // shards
    stages = shards.bit_length() - 1
    tile = 1024
    parts = len(gathered)
    part_rows = size // parts
    pieces_of = len(units)
    where = []
    for piece, unit in enumerate(units):
        where += [(piece, low) for low in range(0, unit.shape[1], size)]

    def kernel(pos_ref, *refs):
        part_refs = refs[:parts]
        unit_refs = refs[parts : parts + pieces_of]
        att_refs = refs[parts + pieces_of : parts + 2 * pieces_of]
        gain_ref, ow_ref, mix_ref, wide_ref, fast_ref = refs[parts + 2 * pieces_of :]

        @pl.when(pl.program_id(0) == 0)
        def _():
            for place in range(shards):
                owner = pos_ref[0] ^ bit_reverse(place, stages)
                low = (place * slab) % part_rows
                rows = part_refs[place * slab // part_rows][low : low + slab, :]
                wide_ref[pl.ds(pl.multiple_of(owner * slab, slab), slab), :] = rows.astype(F32)
            fast_ref[...] = wide_ref[...].astype(BF16)

        pieces = []
        for head in range(heads):
            low = head * 3 * size
            piece, col = where[head]
            cols = slice(col, col + size)
            query = unit_refs[piece][:, cols]
            gate = dot(query, fast_ref[:, low : low + size])
            up = dot(query, fast_ref[:, low + size : low + 2 * size])
            hidden = (gate * jax.nn.sigmoid(gate) * up).astype(BF16)
            out = dot_nt(hidden, fast_ref[:, low + 2 * size : low + 3 * size])
            out = out * lax.rsqrt(jnp.mean(out * out, axis=-1, keepdims=True) + 1e-06)
            normed = (out * gain_ref[head : head + 1, :]).astype(BF16).astype(F32)
            pieces.append((normed + att_refs[piece][:, cols]).astype(BF16))
        combined = jnp.concatenate(pieces, axis=1)
        mix_ref[...] = dot(combined, ow_ref[...]).astype(BF16)

    return pl.pallas_call(
        kernel,
        grid_spec=pltpu.PrefetchScalarGridSpec(
            num_scalar_prefetch=1,
            grid=(tok_dev // tile,),
            in_specs=[pl.BlockSpec((part_rows, 3 * width), lambda i, p: (0, 0))] * parts
            + [pl.BlockSpec((tile, unit.shape[1]), lambda i, p: (i, 0)) for unit in units] * 2
            + [
                pl.BlockSpec((heads, size), lambda i, p: (0, 0)),
                pl.BlockSpec((width, width), lambda i, p: (0, 0)),
            ],
            out_specs=pl.BlockSpec((tile, width), lambda i, p: (i, 0)),
            scratch_shapes=[
                pltpu.VMEM((size, 3 * width), F32),
                pltpu.VMEM((size, 3 * width), BF16),
            ],
        ),
        out_shape=jax.ShapeDtypeStruct((tok_dev, width), BF16),
        compiler_params=params(40),
        cost_estimate=cost(
            2 * tok_dev * width * (width + 3 * size),
            8 * tok_dev * width + 2 * width * width + 6 * size * width,
            tok_dev * width,
        ),
        name="apply_fast",
    )(position, *gathered, *units, *attends, norm_gain, output_weight)


def body(
    activations,
    view_id,
    window_lengths,
    project_weight,
    rate_weight,
    fast_start,
    momentum,
    norm_gain,
    output_weight,
):
    tok_dev, width = activations.shape
    shards = lax.axis_size("tok")
    index = lax.axis_index("tok")
    position = index.reshape(1).astype(jnp.int32)
    heads = rate_weight.shape[1]
    size = width // heads
    slab = size // shards

    def swap(array, bit):
        return lax.ppermute(array, "tok", [(i, i ^ bit) for i in range(shards)])

    sent = group_by_view(view_id, activations, shards)
    arrived = lax.all_to_all(
        sent.reshape(shards, tok_dev // shards, width), "tok", split_axis=0, concat_axis=0, tiled=True
    ).reshape(tok_dev, width)
    ends = jnp.cumsum(window_lengths[0])
    own_start = lax.dynamic_slice_in_dim(fast_start, index * slab, slab, 0)

    keep, send = fast_gradient(
        position, after(activations, sent), project_weight, rate_weight, fast_start, shards
    )
    units, attends = [], []
    bit = 1
    while bit < shards:
        received = swap(send, bit)
        if bit == 2:
            source = after(project_weight, send)
            held = [None] + [head_weights(source, heads, head) for head in range(1, heads)]
            received = after(received, *held[1:])
        if bit == 4:
            held[0] = head_weights(after(project_weight, send), heads, 0)
            received = after(received, held[0])
        if bit == 8:
            unit, attended = project_and_attend(ends, after(arrived, send), held[0])
            units.append(unit)
            attends.append(attended)
            received = after(received, attended)
        bit *= 2
        if bit < shards:
            keep, send = add_and_halve(keep, received)
    momentum_next, block = update_rows(keep, received, momentum, own_start)

    def attend(count, *others):
        first = len(units)
        for head in range(first, min(first + count, heads)):
            unit, attended = project_and_attend(ends, after(arrived, *others), held[head])
            units.append(unit)
            attends.append(attended)

    bit = shards // 2
    while bit > 4:
        attend(1, block)
        block = join(block, after(swap(block, bit), attends[-1]))
        bit //= 2
    attend(1, block)
    own = {0: block, 4: swap(block, 4), 2: swap(block, 2)}
    other = {0: swap(block, 1)}
    last = after(own[4], attends[-1])
    own[6] = swap(last, 2)
    other[4] = swap(last, 1)
    other[2] = swap(after(own[2], attends[-1]), 1)
    attend(heads, last)
    other[6] = swap(after(own[6], attends[-1]), 1)
    gathered = [side[place] for side in (own, other) for place in (0, 4, 2, 6)]
    mixed = apply_fast(position, gathered, units, attends, norm_gain, output_weight, shards)
    return (mixed[None], momentum_next)


def solution(mesh):
    in_specs = (
        P(("group", "tok"), None),
        P(("group", "tok")),
        P(("group", "tok"), None),
        P(),
        P(),
        P(),
        P(("group", "tok"), None, None, None),
        P(),
        P(),
    )
    out_specs = (P(("group", "tok"), None, None), P(("group", "tok"), None, None, None))
    return jax.shard_map(body, mesh=mesh, in_specs=in_specs, out_specs=out_specs, check_vma=False)
```
